256 devices in a mesh: dp: 8 (over z_lo, core), expert: 32 (over x, z_hi, y).
Axes of the slice: x: 4, y: 4, z: 8 (z_hi: 2, z_lo: 4; z = z_hi * 4 + z_lo), core: 2. Of those that a mesh axis runs over, the one named last changes fastest.
Arguments:
- tokens: bfloat16 [16384, 2048], P(('dp', 'expert')), may hold values from -6 to 6
- routes: int32 [16384, 8], P(('dp', 'expert')), may hold values from 0 to 63, all different within a row; in each aligned block of 64 rows (0 to 63, 64 to 127, ...) at most 12 rows name the same one
- route_weight: int32 [16384, 8], P(('dp', 'expert')), may hold values from 1 to 65535
- capacity: int32 [64], replicated, may hold values from 8 to 10
- hot_expert: int32 [1], replicated, may hold values from 0 to 63
- w_gate: bfloat16 [64, 2048, 768], P('expert', 'dp'), may hold values from -0.125 to 0.125
- w_up: bfloat16 [64, 2048, 768], P('expert', 'dp'), may hold values from -0.125 to 0.125
- w_down: bfloat16 [64, 768, 2048], P('expert', None, 'dp'), may hold values from -0.21875 to 0.21875
Outputs:
- mixed: bfloat16 [16384, 2048], P(('dp', 'expert'))
The draws below stay inside these ranges and needn't reach their ends.
All inputs are finite; a program needn't handle non-finite values.
Results may differ from the reference program's by a relative error of at most 0.0057.
Values may be sent and summed in bfloat16 or wider, within the bound.
No kernel may reach another device: no remote copies, remote signals or barrier semaphores. Data moves between devices by JAX's collectives and lax.ppermute only.
A program may use at most 128 MiB of HBM per device.

```python
import math
import jax
import jax.numpy as jnp
import numpy as np
from jax import lax

D = 2048
FF = 768
EXPERTS = 64
TOP = 8
HOT = 1
TOK_DEV = 64
CAP = 10
MOST = 12
TOKENS = 16384


def touch_ends(result, key, smallest, top_value):
    shape = result.shape
    spot = [jax.random.randint(jax.random.fold_in(key, axis), (), 0, shape[axis]) for axis in range(len(shape))]
    result = result.at[tuple(spot)].set(smallest)
    longest = shape.index(max(shape))
    spot[longest] = (spot[longest] + 1) % shape[longest]
    return result.at[tuple(spot)].set(top_value)


def steps_of(own_key, dims, split, least, top_value):
    loudness = 1.0
    for axis_at, blocks in split:
        steps = jax.random.uniform(jax.random.fold_in(jax.random.fold_in(own_key, 6), axis_at), (blocks,), jnp.float32, least / len(split), top_value / len(split))
        loudness = loudness * jnp.repeat(jnp.exp(steps), dims[axis_at] // blocks).reshape((-1,) + (1,) * (len(dims) - 1 - axis_at))
    return loudness


def routed_block(own_key, own, number, rows, amount, top, limit, slope):
    sequence = jax.random.permutation(own_key, amount)
    packed, ordinary = shares(amount, rows * top, limit, slope, True), shares(amount, rows * top, limit, slope, False)
    places = jnp.arange(amount)

    def named(tallies, offset_by):
        used = int((tallies > 0).sum())
        fixed = max(1, used // 4)
        shifted = fixed + (places - fixed + offset_by * (used - fixed)) % max(1, amount - fixed)
        return jnp.zeros((amount,), jnp.int32).at[sequence[jnp.where(places < fixed, places, shifted)]].set(jnp.asarray(tallies, jnp.int32))

    tallies = jnp.where(number % 4 == 0, named(packed, number // 4), named(ordinary, number - number // 4 - 1))
    mixed = jax.random.permutation(jax.random.fold_in(own, 3), amount)
    source_of, sink = mixed[0:amount // 2 * 2:2], mixed[1:amount // 2 * 2:2]
    margin = jnp.minimum(tallies[source_of] - 1, limit - tallies[sink]) // 2
    margin = jnp.where((source_of == sequence[0]) | (sink == sequence[0]) | (tallies[sink] == 0), 0, jnp.maximum(margin, 0))
    shifted = jax.random.randint(jax.random.fold_in(own, 4), (amount // 2,), 0, 1 << 20) % (margin + 1)
    tallies = tallies.at[source_of].add(-shifted).at[sink].add(shifted)
    items = jnp.searchsorted(jnp.cumsum(tallies), jnp.arange(rows * top), side="right").astype(jnp.int32)
    listing = items.reshape(top, rows).T
    listing = listing[jax.random.permutation(jax.random.fold_in(own, 1), rows)]
    offset_by = jax.random.randint(jax.random.fold_in(own, 2), (rows, 1), 0, top)
    return jnp.take_along_axis(listing, (jnp.arange(top)[None, :] + offset_by) % top, axis=1)


def shares(count, total, most, lean, full):
    portions = [(1 << 20) // math.isqrt(rank ** lean) + 1 for rank in range(1, count + 1)]
    largest = most if full else min(most, max(-(-total // count), total * portions[0] // sum(portions)))
    least = 1 if total - largest >= count - 1 else 0
    given, rest = [largest] + [least] * (count - 1), total - largest - least * (count - 1)
    while rest > 0:
        movable = [i for i in range(1, count) if given[i] < largest] or [i for i in range(1, count) if given[i] < most]
        whole, budget = sum([portions[i] for i in movable]), rest
        for i in movable:
            more = min(most - given[i], max(1, budget * portions[i] // whole), rest)
            given[i] = given[i] + more
            rest = rest - more
    return np.array(given)


def centred(rng, extent, deviation, bound, shards=(), kind=jnp.bfloat16):
    factor_of = steps_of(rng, extent, shards, -0.22, 0.18) if shards else 1.0
    result = jax.random.normal(rng, extent, jnp.float32) * deviation * factor_of
    return jnp.minimum(jnp.maximum(result, -bound), bound).astype(kind)


def setup_inputs(seed: int = 0) -> dict:
    arg_keys = jax.random.split(jax.random.key(seed), 9)
    tokens = centred(arg_keys[0], (TOKENS, D), 1.0, 6.0, ((0, 256),))
    routes_keys = jax.random.split(jax.random.fold_in(arg_keys[1], 1), TOKENS // TOK_DEV)
    routes_turns = jax.random.permutation(jax.random.fold_in(arg_keys[1], 3), TOKENS // TOK_DEV)
    routes = jax.vmap(lambda own, number: routed_block(jax.random.fold_in(arg_keys[1], 2), own, number, TOK_DEV, EXPERTS, TOP, MOST, 2))(routes_keys, routes_turns).reshape((TOKENS, TOP))
    route_weight = touch_ends(jax.random.randint(arg_keys[2], (TOKENS, TOP), 1, 65536), jax.random.fold_in(arg_keys[2], 1), 1, 65535).astype(jnp.int32)
    capacity = touch_ends(jax.random.randint(arg_keys[3], (EXPERTS,), CAP * 4 // 5, CAP + 1), jax.random.fold_in(arg_keys[3], 1), CAP * 4 // 5, CAP).astype(jnp.int32)
    hot_expert = jax.random.randint(arg_keys[4], (HOT,), 0, EXPERTS).astype(jnp.int32)
    w_gate = centred(arg_keys[5], (EXPERTS, D, FF), D ** -0.5, 0.125, ((0, 32), (1, 8)))
    w_up = centred(arg_keys[6], (EXPERTS, D, FF), D ** -0.5, 0.125, ((0, 32), (1, 8)))
    w_down = centred(arg_keys[7], (EXPERTS, FF, D), FF ** -0.5, 0.21875, ((0, 32), (2, 8)))
    return dict(tokens=tokens, routes=routes, route_weight=route_weight, capacity=capacity, hot_expert=hot_expert, w_gate=w_gate, w_up=w_up, w_down=w_down)


def expert_ffn(rows, wg, wu, wd):
    gate = jnp.dot(rows, wg, preferred_element_type=jnp.float32)
    up = jnp.dot(rows, wu, preferred_element_type=jnp.float32)
    hidden = (jax.nn.silu(gate) * up).astype(jnp.bfloat16)
    return jnp.dot(hidden, wd, preferred_element_type=jnp.float32).astype(jnp.bfloat16)


def reference(tokens, routes, route_weight, capacity, hot_expert, w_gate, w_up, w_down):
    blocks = TOKENS // TOK_DEV
    weights = route_weight.astype(jnp.float32)
    share = weights / jnp.sum(weights, axis=1, keepdims=True)
    onehot = (routes[:, :, None] == jnp.arange(EXPERTS, dtype=jnp.int32)[None, None, :]).astype(jnp.int32)
    per_token = jnp.sum(onehot, axis=1).reshape(blocks, TOK_DEV, EXPERTS)
    before = (jnp.cumsum(per_token, axis=1) - per_token).reshape(TOKENS, 1, EXPERTS)
    rank = jnp.sum(onehot * before, axis=2).astype(jnp.int32)
    cap_of = jnp.sum(onehot * capacity[None, None, :], axis=2).astype(jnp.int32)
    hot = hot_expert[0]
    is_hot = routes == hot
    kept_cap = jnp.logical_and(jnp.logical_not(is_hot), rank < cap_of)
    token_id = jnp.broadcast_to(jnp.arange(TOKENS, dtype=jnp.int32)[:, None], (TOKENS, TOP))
    block_id = token_id // TOK_DEV
    padded = jnp.concatenate([tokens, jnp.zeros((1, D), tokens.dtype)], axis=0)

    row_e = jnp.where(kept_cap, routes, EXPERTS).reshape(-1)
    row_s = (block_id * CAP + jnp.minimum(rank, CAP - 1)).reshape(-1)
    index_buf = jnp.full((EXPERTS, blocks * CAP), TOKENS, jnp.int32).at[row_e, row_s].set(token_id.reshape(-1), mode="drop")
    coef_buf = jnp.zeros((EXPERTS, blocks * CAP), jnp.float32).at[row_e, row_s].set(share.reshape(-1), mode="drop")

    def step(total, inputs):
        index, coef, wg, wu, wd = inputs
        out = expert_ffn(jnp.take(padded, index, axis=0), wg, wu, wd)
        return total.at[index].add(coef[:, None] * out.astype(jnp.float32), mode="drop"), None

    total = jnp.zeros((TOKENS, D), jnp.float32)
    total, unused = lax.scan(step, total, (index_buf, coef_buf, w_gate, w_up, w_down))

    hot_s = jnp.where(is_hot, block_id * MOST + rank, blocks * MOST).reshape(-1)
    hot_index = jnp.full((blocks * MOST,), TOKENS, jnp.int32).at[hot_s].set(token_id.reshape(-1), mode="drop")
    hot_coef = jnp.zeros((blocks * MOST,), jnp.float32).at[hot_s].set(share.reshape(-1), mode="drop")
    wg = lax.dynamic_index_in_dim(w_gate, hot, 0, keepdims=False)
    wu = lax.dynamic_index_in_dim(w_up, hot, 0, keepdims=False)
    wd = lax.dynamic_index_in_dim(w_down, hot, 0, keepdims=False)
    out = expert_ffn(jnp.take(padded, hot_index, axis=0), wg, wu, wd)
    total = total.at[hot_index].add(hot_coef[:, None] * out.astype(jnp.float32), mode="drop")
    return total.astype(jnp.bfloat16)
```

```python
import functools
import jax
import jax.numpy as jnp
from jax import lax
from jax.sharding import Mesh, PartitionSpec as P
from jax.experimental import pallas as pl
from jax.experimental.pallas import tpu as pltpu

SLOTS = 12
BLOCKS = 4
VMEM_LIMIT = 56 * 1024 * 1024


def slot_table(metas, scal_ref, cap_ref, tok, top, dests):
    base, hot = scal_ref[0], scal_ref[1]
    row = lax.broadcasted_iota(jnp.int32, (dests, tok), 0)
    expert = (row // 4) * 16 + (row % 4) * 2 + base
    earlier = (
        lax.broadcasted_iota(jnp.int32, (tok, tok), 0) < lax.broadcasted_iota(jnp.int32, (tok, tok), 1)
    ).astype(jnp.float32).astype(jnp.bfloat16)
    out = []
    for b, meta in enumerate(metas):
        named = meta[0:1, :] == expert
        for k in range(1, top):
            named = jnp.logical_or(named, meta[k : k + 1, :] == expert)
        named_f = jnp.where(named, 1.0, 0.0)
        rank = jnp.dot(
            named_f.astype(jnp.bfloat16), earlier, preferred_element_type=jnp.float32
        ).astype(jnp.int32)
        limit = jnp.where(expert == hot, SLOTS, cap_ref[...][:, 0:1])
        kept = jnp.logical_and(named, rank < limit)
        out.append(jnp.where(kept, rank + b * SLOTS, -1))
    return out, expert


def select_rows(slots, dests, width):
    per = BLOCKS * SLOTS
    want = lax.broadcasted_iota(jnp.int32, (dests, per, width), 1)
    return want == slots[:, None, :]


def dispatch_kernel(scal_ref, cap_ref, m0, m1, m2, m3, t0, t1, t2, t3, o_ref):
    tok = t0.shape[0]
    dests = o_ref.shape[0]
    top = m0.shape[0] // 2
    slots, unused = slot_table([m[...] for m in (m0, m1, m2, m3)], scal_ref, cap_ref, tok, top, dests)
    slots = jnp.concatenate(slots, axis=1)
    width = t0.shape[1]
    chosen = jnp.where(select_rows(slots, dests, BLOCKS * tok), 1.0, 0.0)
    chosen = chosen.reshape(dests * BLOCKS * SLOTS, BLOCKS * tok).astype(jnp.bfloat16)
    step = 512
    for n in range(0, width, step):
        rows = jnp.concatenate([t[:, n : n + step] for t in (t0, t1, t2, t3)], axis=0)
        got = jnp.dot(chosen, rows, preferred_element_type=jnp.float32).astype(jnp.bfloat16)
        o_ref[:, :, n : n + step] = got.reshape(dests, BLOCKS * SLOTS, step)


def combine_kernel(scal_ref, cap_ref, m0, m1, m2, m3, r_ref, o0, o1, o2, o3):
    tok = o0.shape[0]
    dests = r_ref.shape[0]
    top = m0.shape[0] // 2
    metas = [m[...] for m in (m0, m1, m2, m3)]
    slots, expert = slot_table(metas, scal_ref, cap_ref, tok, top, dests)
    shares = []
    for meta in metas:
        weight = meta[top:, :].astype(jnp.float32)
        share = weight / jnp.sum(weight, axis=0, keepdims=True)
        picked = jnp.zeros((dests, tok), jnp.float32)
        for k in range(top):
            picked = picked + jnp.where(meta[k : k + 1, :] == expert, share[k : k + 1, :], 0.0)
        shares.append(picked)
    slots = jnp.concatenate(slots, axis=1)
    shares = jnp.concatenate(shares, axis=1)
    factor = jnp.where(select_rows(slots, dests, BLOCKS * tok), shares[:, None, :], 0.0)
    factor = factor.reshape(dests * BLOCKS * SLOTS, BLOCKS * tok).T
    high = factor.astype(jnp.bfloat16)
    low = (factor - high.astype(jnp.float32)).astype(jnp.bfloat16)
    width = r_ref.shape[2]
    step = 512
    for n in range(0, width, step):
        rows = r_ref[:, :, n : n + step].reshape(dests * BLOCKS * SLOTS, step)
        part = jnp.dot(high, rows, preferred_element_type=jnp.float32)
        part = part + jnp.dot(low, rows, preferred_element_type=jnp.float32)
        for b, o in enumerate((o0, o1, o2, o3)):
            o[:, n : n + step] = part[b * tok : (b + 1) * tok].astype(o.dtype)


def up_kernel(off_ref, x_ref, *refs):
    gates, ups = refs[0:8], refs[8:16]
    h_ref, wg, wu, sems = refs[16:]
    size = gates[1].shape[0]
    copies = []
    for which, (group, dst) in enumerate(((gates, wg), (ups, wu))):
        for i in range(8):
            src = group[i].at[off_ref[8]] if i == 0 else group[i]
            at = pl.multiple_of(off_ref[i] * size, size)
            copies.append(pltpu.make_async_copy(src, dst.at[pl.ds(at, size), :], sems.at[which * 8 + i]))
    for c in copies:
        c.start()
    for c in copies:
        c.wait()
    rows = x_ref.shape[0]
    step = 128
    for r in range(0, rows, step):
        x = x_ref[r : r + step, :]
        gate = jnp.dot(x, wg[...], preferred_element_type=jnp.float32)
        up = jnp.dot(x, wu[...], preferred_element_type=jnp.float32)
        h_ref[r : r + step, :] = (gate / (1.0 + jnp.exp(-gate)) * up).astype(jnp.bfloat16)


def down_kernel(off_ref, h_ref, *refs):
    downs = refs[0:8]
    o_ref, wd, sems = refs[8:]
    size = downs[1].shape[1]
    copies = []
    for i in range(8):
        src = downs[i].at[off_ref[8]] if i == 0 else downs[i]
        at = pl.multiple_of(off_ref[i] * size, size)
        copies.append(pltpu.make_async_copy(src, wd.at[:, pl.ds(at, size)], sems.at[i]))
    for c in copies:
        c.start()
    for c in copies:
        c.wait()
    rows = h_ref.shape[0]
    step = 128
    for r in range(0, rows, step):
        o_ref[r : r + step, :] = jnp.dot(
            h_ref[r : r + step, :], wd[...], preferred_element_type=jnp.float32
        ).astype(jnp.bfloat16)


def per_device(tokens, routes, route_weight, capacity, hot_expert, w_gate, w_up, w_down):
    zp, zq, core, zh = (lax.axis_index(n) for n in ("zp", "zq", "core", "zh"))
    ring = ("zp", "zh")
    order = [0, 2, 1, 3]
    fwd = [(order[i], order[(i + 1) % 4]) for i in range(4)]
    back = [(order[(i + 1) % 4], order[i]) for i in range(4)]
    opp = [(order[i], order[(i + 2) % 4]) for i in range(4)]
    swap = [(0, 1), (1, 0)]
    tok, width = tokens.shape
    half = tok // 2
    dests = 16
    bf = jnp.bfloat16
    smem = pl.BlockSpec(memory_space=pltpu.SMEM)
    vmem = pl.BlockSpec(memory_space=pltpu.VMEM)
    anym = pl.BlockSpec(memory_space=pl.ANY)
    params = pltpu.CompilerParams(vmem_limit_bytes=VMEM_LIMIT)

    meta0 = jnp.concatenate([routes.T, route_weight.T], axis=0)
    meta1 = lax.ppermute(meta0, ring, fwd)
    meta3 = lax.ppermute(meta0, ring, back)
    meta2 = lax.ppermute(meta0, ring, opp)
    tok1 = lax.ppermute(tokens, ring, fwd)
    tok3 = lax.ppermute(tokens, ring, back)
    tok2 = jnp.concatenate(
        [lax.ppermute(tok1[:half], ring, fwd), lax.ppermute(tok3[half:], ring, back)], axis=0
    )
    metas = (meta0, meta1, meta2, meta3)
    base = zh * 8 + zp
    scal = jnp.stack([base.astype(jnp.int32), hot_expert[0]])
    cap_x = capacity.reshape(4, 2, 4, 2)
    cap_mine = lax.dynamic_index_in_dim(cap_x, zh, 1, keepdims=False)
    cap_mine = lax.dynamic_index_in_dim(cap_mine, zp, 2, keepdims=False).reshape(dests, 1)
    cap_mine = jnp.broadcast_to(cap_mine, (dests, 128))

    per = BLOCKS * SLOTS
    sent = pl.pallas_call(
        dispatch_kernel,
        out_shape=jax.ShapeDtypeStruct((dests, per, width), bf),
        in_specs=[smem] + [vmem] * 9,
        out_specs=vmem,
        compiler_params=params,
        cost_estimate=pl.CostEstimate(
            flops=2 * dests * per * BLOCKS * tok * width, bytes_accessed=4 << 20, transcendentals=0
        ),
        name="dispatch",
    )(scal, cap_mine, *metas, tokens, tok1, tok2, tok3)
    received = lax.all_to_all(sent, ("x", "y"), split_axis=0, concat_axis=0, tiled=True)

    def shards(w):
        mine = lax.dynamic_index_in_dim(w, zp, 0, keepdims=False)
        other = lax.dynamic_index_in_dim(w, 1 - zp, 0, keepdims=False)
        a = lax.ppermute(other, "zp", swap)
        b = lax.ppermute(mine, "zq", swap)
        c = lax.ppermute(a, "zq", swap)
        near = [lax.ppermute(v, "core", swap) for v in (mine, a, b, c)]
        return [w, a, b, c] + near

    gates, ups, downs = shards(w_gate), shards(w_up), shards(w_down)
    place = []
    for g in (0, 1):
        for b in (0, 1):
            for a in (0, 1):
                place.append((zp ^ a) * 4 + (zq ^ b) * 2 + (core ^ g))
    off = jnp.stack(place + [zp]).astype(jnp.int32)
    ff = w_gate.shape[2]
    rows = dests * per
    x = received.reshape(rows, width)
    hidden = pl.pallas_call(
        up_kernel,
        out_shape=jax.ShapeDtypeStruct((rows, ff), bf),
        in_specs=[smem, vmem] + [anym] * 16,
        out_specs=vmem,
        scratch_shapes=[pltpu.VMEM((width, ff), bf)] * 2 + [pltpu.SemaphoreType.DMA((16,))],
        compiler_params=params,
        cost_estimate=pl.CostEstimate(
            flops=4 * rows * width * ff, bytes_accessed=11 << 20, transcendentals=rows * ff
        ),
        name="gate_up",
    )(off, x, *gates, *ups)
    out = pl.pallas_call(
        down_kernel,
        out_shape=jax.ShapeDtypeStruct((rows, width), bf),
        in_specs=[smem, vmem] + [anym] * 8,
        out_specs=vmem,
        scratch_shapes=[pltpu.VMEM((ff, width), bf), pltpu.SemaphoreType.DMA((8,))],
        compiler_params=params,
        cost_estimate=pl.CostEstimate(
            flops=2 * rows * width * ff, bytes_accessed=8 << 20, transcendentals=0
        ),
        name="down",
    )(off, hidden, *downs)
    returned = lax.all_to_all(
        out.reshape(dests, per, width), ("x", "y"), split_axis=0, concat_axis=0, tiled=True
    )
    part0, part1, part2, part3 = pl.pallas_call(
        combine_kernel,
        out_shape=[jax.ShapeDtypeStruct((tok, width), jnp.float32)]
        + [
            jax.ShapeDtypeStruct((tok, width), jnp.float32),
            jax.ShapeDtypeStruct((tok, width), bf),
            jax.ShapeDtypeStruct((tok, width), jnp.float32),
        ],
        in_specs=[smem] + [vmem] * 6,
        out_specs=[vmem] * 4,
        compiler_params=params,
        cost_estimate=pl.CostEstimate(
            flops=4 * dests * per * BLOCKS * tok * width, bytes_accessed=6 << 20, transcendentals=0
        ),
        name="combine",
    )(scal, cap_mine, *metas, returned)
    far_back = lax.ppermute(part2[:half], ring, back)
    far_fwd = lax.ppermute(part2[half:], ring, fwd)
    to_back = jnp.concatenate([part1[:half] + far_back.astype(jnp.float32), part1[half:]], axis=0)
    to_fwd = jnp.concatenate([part3[:half], part3[half:] + far_fwd.astype(jnp.float32)], axis=0)
    from_next = lax.ppermute(to_back.astype(bf), ring, back)
    from_prev = lax.ppermute(to_fwd.astype(bf), ring, fwd)
    total = part0 + from_next.astype(jnp.float32) + from_prev.astype(jnp.float32)
    return total.astype(bf)


def solution(mesh):
    fine = Mesh(mesh.devices.reshape(2, 2, 2, 4, 2, 4), ("zp", "zq", "core", "x", "zh", "y"))
    dp, ex = ("zp", "zq", "core"), ("x", "zh", "y")
    in_specs = (
        P(dp + ex, None),
        P(dp + ex, None),
        P(dp + ex, None),
        P(),
        P(),
        P(ex, dp, None),
        P(ex, dp, None),
        P(ex, None, dp),
    )
    return jax.shard_map(
        per_device, mesh=fine, in_specs=in_specs, out_specs=P(dp + ex, None), check_vma=False
    )
```

```python
import jax
import jax.numpy as jnp
from jax import lax
from jax.sharding import Mesh, PartitionSpec as P
from jax.experimental import pallas as pl
from jax.experimental.pallas import tpu as pltpu

SLOTS = 12
DESTS = 16
TOP = 8
VMEM_LIMIT = 56 * 1024 * 1024
BF = jnp.bfloat16
SMEM = pl.BlockSpec(memory_space=pltpu.SMEM)
VMEM = pl.BlockSpec(memory_space=pltpu.VMEM)
ANY = pl.BlockSpec(memory_space=pl.ANY)
PARAMS = pltpu.CompilerParams(vmem_limit_bytes=VMEM_LIMIT)


def pack_kernel(t_ref, r_ref, w_ref, o_ref):
    half = t_ref.shape[0] // 2
    tok = t_ref.shape[0]
    o_ref[0:half, :] = t_ref[0:half, :]
    o_ref[half + TOP :, :] = t_ref[half:, :]
    weight = w_ref[...]
    high = weight // 256
    low = weight - high * 256
    gap = jnp.zeros((TOP, 128 - tok), jnp.float32)
    parts = []
    for v in (r_ref[...], high, low):
        parts += [v.astype(jnp.float32), gap]
    used = 128 * 3
    o_ref[half : half + TOP, 0:used] = jnp.concatenate(parts, axis=1).astype(BF)
    o_ref[half : half + TOP, used:] = jnp.zeros((TOP, t_ref.shape[1] - used), BF)


def weights_kernel(s_ref, g_ref, u_ref, d_ref, mgu, ogu, md, od, bgu, bd, sem_in, sem_out):
    zp = s_ref[0]
    loads, stores = [], []
    for which in (0, 1):
        e = zp if which == 0 else 1 - zp
        gu_out, d_out = ((mgu, md), (ogu, od))[which]
        for i, src in enumerate((g_ref, u_ref)):
            loads.append(pltpu.make_async_copy(src.at[e], bgu.at[which, i], sem_in.at[which * 3 + i]))
            stores.append(
                pltpu.make_async_copy(bgu.at[which, i], gu_out.at[i], sem_out.at[which * 3 + i])
            )
        loads.append(pltpu.make_async_copy(d_ref.at[e], bd.at[which], sem_in.at[which * 3 + 2]))
        stores.append(pltpu.make_async_copy(bd.at[which], d_out, sem_out.at[which * 3 + 2]))
    for c in loads:
        c.start()
    for a, b in zip(loads, stores):
        a.wait()
        b.start()
    for b in stores:
        b.wait()


def read_meta(ref, half, tok):
    rows = ref[half : half + TOP, 0:384].astype(jnp.float32)
    return rows[:, 0:tok], rows[:, 128 : 128 + tok] * 256.0 + rows[:, 256 : 256 + tok]


def plane_experts(s_ref, cap_ref, hot_ref, tok):
    base = s_ref[1]
    row = lax.broadcasted_iota(jnp.int32, (DESTS, tok), 0)
    expert = (row // 4) * 16 + (row % 4) * 2 + base
    limit = jnp.zeros((DESTS, tok), jnp.int32)
    for d in range(DESTS):
        e = (d // 4) * 16 + (d % 4) * 2 + base
        cap = jnp.where(e == hot_ref[0], SLOTS, cap_ref[e])
        limit = jnp.where(row == d, cap, limit)
    return expert.astype(jnp.float32), limit.astype(jnp.float32)


def slots_of(named_by, expert, limit, first, tok):
    earlier = jnp.where(
        lax.broadcasted_iota(jnp.int32, (tok, tok), 0) < lax.broadcasted_iota(jnp.int32, (tok, tok), 1),
        1.0,
        0.0,
    ).astype(BF)
    named = named_by[0:1, :] == expert
    for k in range(1, TOP):
        named = jnp.logical_or(named, named_by[k : k + 1, :] == expert)
    rank = jnp.dot(jnp.where(named, 1.0, 0.0).astype(BF), earlier, preferred_element_type=jnp.float32)
    kept = jnp.logical_and(named, rank < limit)
    return jnp.where(kept, rank + first, -1.0).astype(jnp.int32)


def match_rows(slots, per, width):
    want = lax.broadcasted_iota(jnp.int32, (DESTS, per, width), 1)
    return want == slots[:, None, :]


def dispatch_kernel(s_ref, cap_ref, hot_ref, *refs):
    o_ref = refs[-1]
    refs = refs[:-1]
    far = len(refs) == 3
    half = 32
    tok = 2 * half
    per = o_ref.shape[1]
    expert, limit = plane_experts(s_ref, cap_ref, hot_ref, tok)
    slots = []
    for b, ref in enumerate(refs[:2]):
        routes, _ = read_meta(ref, half, tok)
        slots.append(slots_of(routes, expert, limit, b * SLOTS, tok))
    slots = jnp.concatenate(slots, axis=1)
    chosen = jnp.where(match_rows(slots, per, 2 * tok), 1.0, 0.0)
    chosen = chosen.reshape(DESTS * per, 2 * tok).astype(BF)
    width = o_ref.shape[2]
    step = 512
    for n in range(0, width, step):
        at = slice(n, n + step)
        rows = []
        for b, ref in enumerate(refs[:2]):
            rows.append(ref[0:half, at])
            if far and b == 1:
                rows.append(refs[2][:, at])
            else:
                rows.append(ref[half + TOP :, at])
        got = jnp.dot(chosen, jnp.concatenate(rows, axis=0), preferred_element_type=jnp.float32)
        o_ref[:, :, at] = got.astype(BF).reshape(DESTS, per, step)


def factors(s_ref, cap_ref, hot_ref, refs, per, half):
    tok = 2 * half
    expert, limit = plane_experts(s_ref, cap_ref, hot_ref, tok)
    slots, shares = [], []
    for b, ref in enumerate(refs):
        routes, weight = read_meta(ref, half, tok)
        slots.append(slots_of(routes, expert, limit, b * SLOTS, tok))
        share = weight / jnp.sum(weight, axis=0, keepdims=True)
        picked = jnp.zeros((DESTS, tok), jnp.float32)
        for k in range(TOP):
            picked = picked + jnp.where(routes[k : k + 1, :] == expert, share[k : k + 1, :], 0.0)
        shares.append(picked)
    slots = jnp.concatenate(slots, axis=1)
    shares = jnp.concatenate(shares, axis=1)
    factor = jnp.where(match_rows(slots, per, 2 * tok), shares[:, None, :], 0.0)
    factor = factor.reshape(DESTS * per, 2 * tok).T
    high = factor.astype(BF)
    low = (factor - high.astype(jnp.float32)).astype(BF)
    return high, low


def combine_kernel(s_ref, cap_ref, hot_ref, ta, tb, r_ref, *outs):
    half = 32
    per, width = r_ref.shape[1], r_ref.shape[2]
    high, low = factors(s_ref, cap_ref, hot_ref, (ta, tb), per, half)
    step = 512
    for n in range(0, width, step):
        rows = r_ref[:, :, n : n + step].reshape(DESTS * per, step)
        part = jnp.dot(high, rows, preferred_element_type=jnp.float32)
        part = part + jnp.dot(low, rows, preferred_element_type=jnp.float32)
        for i, o in enumerate(outs):
            o[:, n : n + step] = part[i * half : (i + 1) * half].astype(o.dtype)


def up_kernel(off_ref, xa_ref, xb_ref, *refs):
    groups = refs[0:8]
    ha_ref, hb_ref, wg, wu, gate_s, sems = refs[8:]
    size = groups[0].shape[1]
    copies = [[], []]
    for which, dst in enumerate((wg, wu)):
        for i in range(8):
            at = pl.multiple_of(off_ref[i] * size, size)
            copies[which].append(
                pltpu.make_async_copy(
                    groups[i].at[which], dst.at[pl.ds(at, size), :], sems.at[which * 8 + i]
                )
            )
    for group in copies:
        for c in group:
            c.start()
    rows = xa_ref.shape[0]
    step = 128
    for c in copies[0]:
        c.wait()
    for j, x_ref in enumerate((xa_ref, xb_ref)):
        for r in range(0, rows, step):
            gate_s[j * rows + r : j * rows + r + step, :] = jnp.dot(
                x_ref[r : r + step, :], wg[...], preferred_element_type=jnp.float32
            )
    for c in copies[1]:
        c.wait()
    for j, (x_ref, h_ref) in enumerate(((xa_ref, ha_ref), (xb_ref, hb_ref))):
        for r in range(0, rows, step):
            gate = gate_s[j * rows + r : j * rows + r + step, :]
            up = jnp.dot(x_ref[r : r + step, :], wu[...], preferred_element_type=jnp.float32)
            h_ref[r : r + step, :] = (gate / (1.0 + jnp.exp(-gate)) * up).astype(BF)


def down_kernel(off_ref, h_ref, *refs):
    downs = refs[0:8]
    o_ref, wd, sems = refs[8:]
    size = downs[0].shape[1]
    copies = []
    for i in range(8):
        at = pl.multiple_of(off_ref[i] * size, size)
        copies.append(pltpu.make_async_copy(downs[i], wd.at[:, pl.ds(at, size)], sems.at[i]))
    for c in copies:
        c.start()
    for c in copies:
        c.wait()
    rows = h_ref.shape[0]
    step = 128
    for r in range(0, rows, step):
        o_ref[r : r + step, :] = jnp.dot(
            h_ref[r : r + step, :], wd[...], preferred_element_type=jnp.float32
        ).astype(BF)


def cost(flops, moved, hard=0):
    return pl.CostEstimate(flops=flops, bytes_accessed=moved, transcendentals=hard)


def shape(dims, kind=BF):
    return jax.ShapeDtypeStruct(dims, kind)


def exchange(value):
    return lax.all_to_all(value, ("x", "y"), split_axis=0, concat_axis=0, tiled=True)


def per_device(tokens, routes, route_weight, capacity, hot_expert, w_gate, w_up, w_down):
    zp, zq, core, zh = (lax.axis_index(n) for n in ("zp", "zq", "core", "zh"))
    ring = ("zp", "zh")
    order = [0, 2, 1, 3]
    fwd = [(order[i], order[(i + 1) % 4]) for i in range(4)]
    back = [(order[(i + 1) % 4], order[i]) for i in range(4)]
    swap = [(0, 1), (1, 0)]
    tok, width = tokens.shape
    half = tok // 2
    ff = w_gate.shape[2]
    piece = w_gate.shape[1]
    per = 2 * SLOTS
    rows = DESTS * per
    split = half + TOP

    own = pl.pallas_call(
        pack_kernel,
        out_shape=shape((tok + TOP, width)),
        in_specs=[VMEM] * 3,
        out_specs=VMEM,
        compiler_params=PARAMS,
        cost_estimate=cost(0, 600 << 10),
        name="pack",
    )(tokens, routes.T, route_weight.T)
    tok1 = lax.ppermute(own, ring, fwd)
    tok3 = lax.ppermute(own, ring, back)

    scal = jnp.stack([zp, zh * 8 + zp]).astype(jnp.int32)
    mine_gu, other_gu, mine_d, other_d = pl.pallas_call(
        weights_kernel,
        out_shape=[shape((2, piece, ff)), shape((2, piece, ff)), shape((ff, piece)), shape((ff, piece))],
        in_specs=[SMEM, ANY, ANY, ANY],
        out_specs=[ANY] * 4,
        scratch_shapes=[
            pltpu.VMEM((2, 2, piece, ff), BF),
            pltpu.VMEM((2, ff, piece), BF),
            pltpu.SemaphoreType.DMA((6,)),
            pltpu.SemaphoreType.DMA((6,)),
        ],
        compiler_params=PARAMS,
        cost_estimate=cost(0, 5 << 20),
        name="pack_weights",
    )(scal, w_gate, w_up, w_down)

    def shards(mine, other):
        a = lax.ppermute(other, "zp", swap)
        b = lax.ppermute(mine, "zq", swap)
        c = lax.ppermute(a, "zq", swap)
        near = [lax.ppermute(v, "core", swap) for v in (mine, a, b, c)]
        return [mine, a, b, c] + near

    gates_ups = shards(mine_gu, other_gu)
    downs = shards(mine_d, other_d)

    far_top = lax.ppermute(tok1[:split], ring, fwd)
    far_low = lax.ppermute(tok3[split:], ring, back)

    def dispatch(*blocks):
        return pl.pallas_call(
            dispatch_kernel,
            out_shape=shape((DESTS, per, width)),
            in_specs=[SMEM] * 3 + [VMEM] * len(blocks),
            out_specs=VMEM,
            compiler_params=PARAMS,
            cost_estimate=cost(2 * rows * 2 * tok * width, 2 << 20),
        )(scal, capacity, hot_expert, *blocks)

    sent_b = dispatch(own, tok3)
    x_b = exchange(sent_b).reshape(rows, width)
    sent_a = dispatch(tok1, far_top, far_low)
    x_a = exchange(sent_a).reshape(rows, width)

    place = []
    for g in (0, 1):
        for b in (0, 1):
            for a in (0, 1):
                place.append((zp ^ a) * 4 + (zq ^ b) * 2 + (core ^ g))
    off = jnp.stack(place).astype(jnp.int32)
    h_a, h_b = pl.pallas_call(
        up_kernel,
        out_shape=[shape((rows, ff))] * 2,
        in_specs=[SMEM, VMEM, VMEM] + [ANY] * 8,
        out_specs=[VMEM] * 2,
        scratch_shapes=[pltpu.VMEM((width, ff), BF)] * 2
        + [pltpu.VMEM((2 * rows, ff), jnp.float32), pltpu.SemaphoreType.DMA((16,))],
        compiler_params=PARAMS,
        cost_estimate=cost(8 * rows * width * ff, 11 << 20, 2 * rows * ff),
        name="gate_up",
    )(off, x_a, x_b, *gates_ups)

    def down(h):
        out = pl.pallas_call(
            down_kernel,
            out_shape=shape((rows, width)),
            in_specs=[SMEM, VMEM] + [ANY] * 8,
            out_specs=VMEM,
            scratch_shapes=[pltpu.VMEM((ff, width), BF), pltpu.SemaphoreType.DMA((8,))],
            compiler_params=PARAMS,
            cost_estimate=cost(2 * rows * width * ff, 6 << 20),
        )(off, h, *downs)
        return out.reshape(DESTS, per, width)

    def combine(ta, tb, got, kinds):
        return pl.pallas_call(
            combine_kernel,
            out_shape=[shape((half, width), k) for k in kinds],
            in_specs=[SMEM] * 3 + [VMEM] * 3,
            out_specs=[VMEM] * len(kinds),
            compiler_params=PARAMS,
            cost_estimate=cost(4 * rows * 2 * tok * width, 3 << 20),
        )(scal, capacity, hot_expert, ta, tb, got)

    f32 = jnp.float32
    back_a = exchange(down(h_a))
    back_b = exchange(down(h_b))
    p1_top, p1_low, p2_top, p2_low = combine(tok1, far_top, back_a, (f32, BF, BF, BF))
    over_back = lax.ppermute(p2_top, ring, back)
    over_fwd = lax.ppermute(p2_low, ring, fwd)
    to_back = jnp.concatenate([(p1_top + over_back.astype(f32)).astype(BF), p1_low], axis=0)
    from_next = lax.ppermute(to_back, ring, back)
    p0_top, p0_low, p3_top, p3_low = combine(own, tok3, back_b, (f32, f32, BF, f32))
    to_fwd = jnp.concatenate([p3_top, (p3_low + over_fwd.astype(f32)).astype(BF)], axis=0)
    from_prev = lax.ppermute(to_fwd, ring, fwd)
    part0 = jnp.concatenate([p0_top, p0_low], axis=0)
    total = part0 + from_next.astype(f32) + from_prev.astype(f32)
    return total.astype(BF)


def solution(mesh):
    fine = Mesh(mesh.devices.reshape(2, 2, 2, 4, 2, 4), ("zp", "zq", "core", "x", "zh", "y"))
    dp, ex = ("zp", "zq", "core"), ("x", "zh", "y")
    in_specs = (
        P(dp + ex, None),
        P(dp + ex, None),
        P(dp + ex, None),
        P(),
        P(),
        P(ex, dp, None),
        P(ex, dp, None),
        P(ex, None, dp),
    )

    return jax.shard_map(
        per_device, mesh=fine, in_specs=in_specs, out_specs=P(dp + ex, None), check_vma=False
    )
```

```python
import jax
import jax.numpy as jnp
from jax import lax
from jax.sharding import Mesh, PartitionSpec as P
from jax.experimental import pallas as pl
from jax.experimental.pallas import tpu as pltpu

SLOTS = 12
DESTS = 16
TOP = 8
BF = jnp.bfloat16
SMEM = pl.BlockSpec(memory_space=pltpu.SMEM)
VMEM = pl.BlockSpec(memory_space=pltpu.VMEM)
ANY = pl.BlockSpec(memory_space=pl.ANY)


def grant(mib):
    return pltpu.CompilerParams(vmem_limit_bytes=mib << 20)


def pack_kernel(
    s_ref, t_ref, r_ref, w_ref, g_ref, u_ref, d_ref, o_ref, mgu, ogu, md, od, bgu, bd, sem_in, sem_out
):
    zp = s_ref[0]
    loads, stores = [], []
    for which in (1, 0):
        e = zp if which == 0 else 1 - zp
        gu_out, d_out = ((mgu, md), (ogu, od))[which]
        for i, src in enumerate((g_ref, u_ref)):
            loads.append(pltpu.make_async_copy(src.at[e], bgu.at[which, i], sem_in.at[which * 3 + i]))
            stores.append(
                pltpu.make_async_copy(bgu.at[which, i], gu_out.at[i], sem_out.at[which * 3 + i])
            )
        loads.append(pltpu.make_async_copy(d_ref.at[e], bd.at[which], sem_in.at[which * 3 + 2]))
        stores.append(pltpu.make_async_copy(bd.at[which], d_out, sem_out.at[which * 3 + 2]))
    for c in loads:
        c.start()
    half = t_ref.shape[0] // 2
    tok = t_ref.shape[0]
    o_ref[0:half, :] = t_ref[0:half, :]
    o_ref[half + TOP :, :] = t_ref[half:, :]
    weight = w_ref[...]
    high = weight // 256
    low = weight - high * 256
    gap = jnp.zeros((TOP, 128 - tok), jnp.float32)
    parts = []
    for v in (r_ref[...], high, low):
        parts += [v.astype(jnp.float32), gap]
    used = 128 * 3
    o_ref[half : half + TOP, 0:used] = jnp.concatenate(parts, axis=1).astype(BF)
    o_ref[half : half + TOP, used:] = jnp.zeros((TOP, t_ref.shape[1] - used), BF)
    for a, b in zip(loads, stores):
        a.wait()
        b.start()
    for b in stores:
        b.wait()


def read_meta(ref, half, tok):
    rows = ref[half : half + TOP, 0:384].astype(jnp.float32)
    return rows[:, 0:tok], rows[:, 128 : 128 + tok] * 256.0 + rows[:, 256 : 256 + tok]


def plane_experts(s_ref, cap_ref, hot_ref, tok):
    base = s_ref[1]
    row = lax.broadcasted_iota(jnp.int32, (DESTS, tok), 0)
    expert = (row // 4) * 16 + (row % 4) * 2 + base
    limit = jnp.zeros((DESTS, tok), jnp.int32)
    for d in range(DESTS):
        e = (d // 4) * 16 + (d % 4) * 2 + base
        cap = jnp.where(e == hot_ref[0], SLOTS, cap_ref[e])
        limit = jnp.where(row == d, cap, limit)
    return expert.astype(jnp.float32), limit.astype(jnp.float32)


def slots_of(named_by, expert, limit, first, tok):
    earlier = jnp.where(
        lax.broadcasted_iota(jnp.int32, (tok, tok), 0) < lax.broadcasted_iota(jnp.int32, (tok, tok), 1),
        1.0,
        0.0,
    ).astype(BF)
    named = named_by[0:1, :] == expert
    for k in range(1, TOP):
        named = jnp.logical_or(named, named_by[k : k + 1, :] == expert)
    rank = jnp.dot(jnp.where(named, 1.0, 0.0).astype(BF), earlier, preferred_element_type=jnp.float32)
    kept = jnp.logical_and(named, rank < limit)
    return jnp.where(kept, rank + first, -1.0).astype(jnp.int32)


def match_rows(slots, per, width):
    want = lax.broadcasted_iota(jnp.int32, (DESTS, per, width), 1)
    return want == slots[:, None, :]


def dispatch_kernel(s_ref, cap_ref, hot_ref, *refs):
    o_ref, f_ref = refs[-2:]
    refs = refs[:-2]
    far = len(refs) == 3
    half = 32
    tok = 2 * half
    per = o_ref.shape[1]
    expert, limit = plane_experts(s_ref, cap_ref, hot_ref, tok)
    slots, shares = [], []
    for b, ref in enumerate(refs[:2]):
        routes, weight = read_meta(ref, half, tok)
        slots.append(slots_of(routes, expert, limit, b * SLOTS, tok))
        share = weight / jnp.sum(weight, axis=0, keepdims=True)
        picked = jnp.zeros((DESTS, tok), jnp.float32)
        for k in range(TOP):
            picked = picked + jnp.where(routes[k : k + 1, :] == expert, share[k : k + 1, :], 0.0)
        shares.append(picked)
    slots = jnp.concatenate(slots, axis=1)
    shares = jnp.concatenate(shares, axis=1)
    match = match_rows(slots, per, 2 * tok)
    chosen = jnp.where(match, 1.0, 0.0).reshape(DESTS * per, 2 * tok).astype(BF)
    factor = jnp.where(match, shares[:, None, :], 0.0).reshape(DESTS * per, 2 * tok).T
    high = factor.astype(BF)
    f_ref[0] = high
    f_ref[1] = (factor - high.astype(jnp.float32)).astype(BF)
    width = o_ref.shape[2]
    step = 512
    for n in range(0, width, step):
        at = slice(n, n + step)
        rows = []
        for b, ref in enumerate(refs[:2]):
            rows.append(ref[0:half, at])
            if far and b == 1:
                rows.append(refs[2][:, at])
            else:
                rows.append(ref[half + TOP :, at])
        got = jnp.dot(chosen, jnp.concatenate(rows, axis=0), preferred_element_type=jnp.float32)
        o_ref[:, :, at] = got.astype(BF).reshape(DESTS, per, step)


def combine_a_kernel(f_ref, r_ref, a_top, a_low, b_top, b_low):
    half = 32
    per, width = r_ref.shape[1], r_ref.shape[2]
    step = 512
    for n in range(0, width, step):
        rows = r_ref[:, :, n : n + step].reshape(DESTS * per, step)
        part = jnp.dot(f_ref[0], rows, preferred_element_type=jnp.float32)
        part = part + jnp.dot(f_ref[1], rows, preferred_element_type=jnp.float32)
        for i, o in enumerate((a_top, a_low, b_top, b_low)):
            o[:, n : n + step] = part[i * half : (i + 1) * half].astype(o.dtype)


def combine_b_kernel(f_ref, r_ref, over_ref, own_ref, out_ref):
    half = 32
    per, width = r_ref.shape[1], r_ref.shape[2]
    step = 512
    for n in range(0, width, step):
        at = slice(n, n + step)
        rows = r_ref[:, :, at].reshape(DESTS * per, step)
        part = jnp.dot(f_ref[0], rows, preferred_element_type=jnp.float32)
        part = part + jnp.dot(f_ref[1], rows, preferred_element_type=jnp.float32)
        own_ref[:, at] = part[0 : 2 * half]
        out_ref[0:half, at] = part[2 * half : 3 * half].astype(BF)
        out_ref[half:, at] = (part[3 * half :] + over_ref[:, at].astype(jnp.float32)).astype(BF)


def join_kernel(top_ref, low_ref, over_ref, out_ref):
    half = top_ref.shape[0]
    out_ref[0:half, :] = (top_ref[...] + over_ref[...].astype(jnp.float32)).astype(BF)
    out_ref[half:, :] = low_ref[...]


def up_kernel(off_ref, xa_ref, xb_ref, *refs):
    groups = refs[0:8]
    ha_ref, hb_ref, wg, wu, gate_s, sems = refs[8:]
    size = groups[0].shape[1]
    copies = [[], []]
    for which, dst in enumerate((wg, wu)):
        for i in range(8):
            at = pl.multiple_of(off_ref[i] * size, size)
            copies[which].append(
                pltpu.make_async_copy(
                    groups[i].at[which], dst.at[pl.ds(at, size), :], sems.at[which * 8 + i]
                )
            )
    for group in copies:
        for c in group:
            c.start()
    rows = xa_ref.shape[0]
    step = 128
    for c in copies[0]:
        c.wait()
    for j, x_ref in enumerate((xa_ref, xb_ref)):
        for r in range(0, rows, step):
            gate_s[j * rows + r : j * rows + r + step, :] = jnp.dot(
                x_ref[r : r + step, :], wg[...], preferred_element_type=jnp.float32
            )
    for c in copies[1]:
        c.wait()
    for j, (x_ref, h_ref) in enumerate(((xa_ref, ha_ref), (xb_ref, hb_ref))):
        for r in range(0, rows, step):
            gate = gate_s[j * rows + r : j * rows + r + step, :]
            up = jnp.dot(x_ref[r : r + step, :], wu[...], preferred_element_type=jnp.float32)
            h_ref[r : r + step, :] = (gate / (1.0 + jnp.exp(-gate)) * up).astype(BF)


def down_kernel(off_ref, h_ref, *refs):
    downs = refs[0:8]
    o_ref, wd, sems = refs[8:]
    size = downs[0].shape[1]
    copies = [pltpu.make_async_copy(downs[i], wd.at[i], sems.at[i]) for i in range(8)]
    for c in copies:
        c.start()
    rows = h_ref.shape[0]
    step = 128
    for i in range(8):
        copies[i].wait()
        at = pl.ds(pl.multiple_of(off_ref[i] * size, size), size)
        for r in range(0, rows, step):
            o_ref[r : r + step, at] = jnp.dot(
                h_ref[r : r + step, :], wd[i], preferred_element_type=jnp.float32
            ).astype(BF)


def cost(flops, moved, hard=0):
    return pl.CostEstimate(flops=flops, bytes_accessed=moved, transcendentals=hard)


def shape(dims, kind=BF):
    return jax.ShapeDtypeStruct(dims, kind)


def exchange(value):
    return lax.all_to_all(value, ("x", "y"), split_axis=0, concat_axis=0, tiled=True)


def per_device(tokens, routes, route_weight, capacity, hot_expert, w_gate, w_up, w_down):
    zp, zq, core, zh = (lax.axis_index(n) for n in ("zp", "zq", "core", "zh"))
    ring = ("zp", "zh")
    order = [0, 2, 1, 3]
    fwd = [(order[i], order[(i + 1) % 4]) for i in range(4)]
    back = [(order[(i + 1) % 4], order[i]) for i in range(4)]
    swap = [(0, 1), (1, 0)]
    tok, width = tokens.shape
    half = tok // 2
    ff = w_gate.shape[2]
    piece = w_gate.shape[1]
    per = 2 * SLOTS
    rows = DESTS * per
    split = half + TOP

    scal = jnp.stack([zp, zh * 8 + zp]).astype(jnp.int32)
    own, mine_gu, other_gu, mine_d, other_d = pl.pallas_call(
        pack_kernel,
        out_shape=[
            shape((tok + TOP, width)),
            shape((2, piece, ff)),
            shape((2, piece, ff)),
            shape((ff, piece)),
            shape((ff, piece)),
        ],
        in_specs=[SMEM] + [VMEM] * 3 + [ANY] * 3,
        out_specs=[VMEM] + [ANY] * 4,
        scratch_shapes=[
            pltpu.VMEM((2, 2, piece, ff), BF),
            pltpu.VMEM((2, ff, piece), BF),
            pltpu.SemaphoreType.DMA((6,)),
            pltpu.SemaphoreType.DMA((6,)),
        ],
        compiler_params=grant(56),
        cost_estimate=cost(0, 5 << 20),
        name="pack",
    )(scal, tokens, routes.T, route_weight.T, w_gate, w_up, w_down)
    tok3 = lax.ppermute(own, ring, back)
    tok1 = lax.ppermute(own, ring, fwd)

    def shards(mine, other):
        a = lax.ppermute(other, "zp", swap)
        b = lax.ppermute(mine, "zq", swap)
        c = lax.ppermute(a, "zq", swap)
        near = [lax.ppermute(v, "core", swap) for v in (mine, a, b, c)]
        return [mine, a, b, c] + near

    gates_ups = shards(mine_gu, other_gu)
    downs = shards(mine_d, other_d)

    far_top = lax.ppermute(tok1[:split], ring, fwd)
    far_low = lax.ppermute(tok3[split:], ring, back)

    def dispatch(*blocks):
        return pl.pallas_call(
            dispatch_kernel,
            out_shape=[shape((DESTS, per, width)), shape((2, 2 * tok, rows))],
            in_specs=[SMEM] * 3 + [VMEM] * len(blocks),
            out_specs=[VMEM] * 2,
            compiler_params=grant(12),
            cost_estimate=cost(2 * rows * 2 * tok * width, 2 << 20),
        )(scal, capacity, hot_expert, *blocks)

    sent_b, fac_b = dispatch(own, tok3)
    x_b = exchange(sent_b).reshape(rows, width)
    sent_a, fac_a = dispatch(tok1, far_top, far_low)
    x_a = exchange(sent_a).reshape(rows, width)

    place = []
    for g in (0, 1):
        for b in (0, 1):
            for a in (0, 1):
                place.append((zp ^ a) * 4 + (zq ^ b) * 2 + (core ^ g))
    off = jnp.stack(place).astype(jnp.int32)
    h_a, h_b = pl.pallas_call(
        up_kernel,
        out_shape=[shape((rows, ff))] * 2,
        in_specs=[SMEM, VMEM, VMEM] + [ANY] * 8,
        out_specs=[VMEM] * 2,
        scratch_shapes=[pltpu.VMEM((width, ff), BF)] * 2
        + [pltpu.VMEM((2 * rows, ff), jnp.float32), pltpu.SemaphoreType.DMA((16,))],
        compiler_params=grant(24),
        cost_estimate=cost(8 * rows * width * ff, 11 << 20, 2 * rows * ff),
        name="gate_up",
    )(off, x_a, x_b, *gates_ups)

    def down(h):
        out = pl.pallas_call(
            down_kernel,
            out_shape=shape((rows, width)),
            in_specs=[SMEM, VMEM] + [ANY] * 8,
            out_specs=VMEM,
            scratch_shapes=[pltpu.VMEM((8, ff, piece), BF), pltpu.SemaphoreType.DMA((8,))],
            compiler_params=grant(12),
            cost_estimate=cost(2 * rows * width * ff, 6 << 20),
        )(off, h, *downs)
        return out.reshape(DESTS, per, width)

    def combine(kernel, ins, outs):
        return pl.pallas_call(
            kernel,
            out_shape=outs,
            in_specs=[VMEM] * len(ins),
            out_specs=[VMEM] * len(outs),
            compiler_params=grant(14),
            cost_estimate=cost(4 * rows * 2 * tok * width, 3 << 20),
        )(*ins)

    f32 = jnp.float32
    back_a = exchange(down(h_a))
    back_b = exchange(down(h_b))
    p1_top, p1_low, p2_top, p2_low = combine(
        combine_a_kernel, (fac_a, back_a), [shape((half, width), k) for k in (f32, BF, BF, BF)]
    )
    over_back = lax.ppermute(p2_top, ring, back)
    over_fwd = lax.ppermute(p2_low, ring, fwd)
    to_back = pl.pallas_call(
        join_kernel,
        out_shape=shape((tok, width)),
        in_specs=[VMEM] * 3,
        out_specs=VMEM,
        compiler_params=grant(8),
        cost_estimate=cost(0, 700 << 10),
        name="join",
    )(p1_top, p1_low, over_back)
    from_next = lax.ppermute(to_back, ring, back)
    part0, to_fwd = combine(
        combine_b_kernel, (fac_b, back_b, over_fwd), [shape((tok, width), f32), shape((tok, width))]
    )
    from_prev = lax.ppermute(to_fwd, ring, fwd)
    total = part0 + from_next.astype(f32) + from_prev.astype(f32)
    return total.astype(BF)


def solution(mesh):
    fine = Mesh(mesh.devices.reshape(2, 2, 2, 4, 2, 4), ("zp", "zq", "core", "x", "zh", "y"))
    dp, ex = ("zp", "zq", "core"), ("x", "zh", "y")
    in_specs = (
        P(dp + ex, None),
        P(dp + ex, None),
        P(dp + ex, None),
        P(),
        P(),
        P(ex, dp, None),
        P(ex, dp, None),
        P(ex, None, dp),
    )

    return jax.shard_map(
        per_device, mesh=fine, in_specs=in_specs, out_specs=P(dp + ex, None), check_vma=False
    )
```

```python
import functools
import jax
import jax.numpy as jnp
from jax import lax
from jax.sharding import Mesh, PartitionSpec as P
from jax.experimental import pallas as pl
from jax.experimental.pallas import tpu as pltpu

SLOTS = 12
EARLY = 4
LATE = SLOTS - EARLY
DESTS = 16
TOP = 8
BF = jnp.bfloat16
SMEM = pl.BlockSpec(memory_space=pltpu.SMEM)
VMEM = pl.BlockSpec(memory_space=pltpu.VMEM)
ANY = pl.BlockSpec(memory_space=pl.ANY)


def grant(mib):
    return pltpu.CompilerParams(vmem_limit_bytes=mib << 20)


def pack_kernel(t_ref, r_ref, w_ref, o_ref):
    half = t_ref.shape[0] // 2
    tok = t_ref.shape[0]
    o_ref[0:half, :] = t_ref[0:half, :]
    o_ref[half + TOP :, :] = t_ref[half:, :]
    weight = w_ref[...]
    high = weight // 256
    low = weight - high * 256
    gap = jnp.zeros((TOP, 128 - tok), jnp.float32)
    parts = []
    for v in (r_ref[...], high, low):
        parts += [v.astype(jnp.float32), gap]
    used = 128 * 3
    o_ref[half : half + TOP, 0:used] = jnp.concatenate(parts, axis=1).astype(BF)
    o_ref[half : half + TOP, used:] = jnp.zeros((TOP, t_ref.shape[1] - used), BF)


def weights_kernel(s_ref, g_ref, u_ref, d_ref, mgu, ogu, md, od, bgu, bd, sem_in, sem_out):
    zp = s_ref[0]
    loads, stores = [], []
    for which in (0, 1):
        e = zp if which == 0 else 1 - zp
        gu_out, d_out = ((mgu, md), (ogu, od))[which]
        for i, src in enumerate((g_ref, u_ref)):
            loads.append(pltpu.make_async_copy(src.at[e], bgu.at[which, i], sem_in.at[which * 3 + i]))
            stores.append(
                pltpu.make_async_copy(bgu.at[which, i], gu_out.at[i], sem_out.at[which * 3 + i])
            )
        loads.append(pltpu.make_async_copy(d_ref.at[e], bd.at[which], sem_in.at[which * 3 + 2]))
        stores.append(pltpu.make_async_copy(bd.at[which], d_out, sem_out.at[which * 3 + 2]))
    for c in loads:
        c.start()
    for a, b in zip(loads, stores):
        a.wait()
        b.start()
    for b in stores:
        b.wait()


def read_meta(ref, half, tok):
    rows = ref[half : half + TOP, 0:384].astype(jnp.float32)
    return rows[:, 0:tok], rows[:, 128 : 128 + tok] * 256.0 + rows[:, 256 : 256 + tok]


def plane_experts(s_ref, cap_ref, hot_ref, tok):
    base = s_ref[1]
    row = lax.broadcasted_iota(jnp.int32, (DESTS, tok), 0)
    expert = (row // 4) * 16 + (row % 4) * 2 + base
    limit = jnp.zeros((DESTS, tok), jnp.int32)
    for d in range(DESTS):
        e = (d // 4) * 16 + (d % 4) * 2 + base
        cap = jnp.where(e == hot_ref[0], SLOTS, cap_ref[e])
        limit = jnp.where(row == d, cap, limit)
    return expert.astype(jnp.float32), limit.astype(jnp.float32)


def slots_of(named_by, expert, limit, first, tok, turn=0):
    earlier = jnp.where(
        lax.broadcasted_iota(jnp.int32, (tok, tok), 0) < lax.broadcasted_iota(jnp.int32, (tok, tok), 1),
        1.0,
        0.0,
    ).astype(BF)
    named = named_by[0:1, :] == expert
    for k in range(1, TOP):
        named = jnp.logical_or(named, named_by[k : k + 1, :] == expert)
    rank = jnp.dot(jnp.where(named, 1.0, 0.0).astype(BF), earlier, preferred_element_type=jnp.float32)
    kept = jnp.logical_and(named, rank < limit)
    if turn:
        rank = jnp.where(rank < turn, rank + (SLOTS - turn), rank - turn)
    return jnp.where(kept, rank + first, -1.0).astype(jnp.int32)


def match_rows(slots, per, width):
    want = lax.broadcasted_iota(jnp.int32, (DESTS, per, width), 1)
    return want == slots[:, None, :]


def dispatch_kernel(far, s_ref, cap_ref, hot_ref, *refs):
    blocks = 3 if far else 2
    o_ref, factor_refs = refs[blocks], refs[blocks + 1 :]
    refs = refs[:blocks]
    half = 32
    tok = 2 * half
    per = o_ref.shape[1]
    expert, limit = plane_experts(s_ref, cap_ref, hot_ref, tok)
    slots, shares = [], []
    for b, ref in enumerate(refs[:2]):
        routes, weight = read_meta(ref, half, tok)
        turn = EARLY if b == 0 and not far else 0
        slots.append(slots_of(routes, expert, limit, b * SLOTS, tok, turn))
        share = weight / jnp.sum(weight, axis=0, keepdims=True)
        picked = jnp.zeros((DESTS, tok), jnp.float32)
        for k in range(TOP):
            picked = picked + jnp.where(routes[k : k + 1, :] == expert, share[k : k + 1, :], 0.0)
        shares.append(picked)
    slots = jnp.concatenate(slots, axis=1)
    shares = jnp.concatenate(shares, axis=1)
    match = match_rows(slots, per, 2 * tok)
    chosen = jnp.where(match, 1.0, 0.0).reshape(DESTS * per, 2 * tok).astype(BF)
    factor = jnp.where(match, shares[:, None, :], 0.0)
    if far:
        pieces = [factor]
    else:
        pieces = [factor[:, LATE:, :], factor[:, 0:LATE, 0:tok]]
    for piece, f_ref in zip(pieces, factor_refs):
        piece = piece.reshape(-1, piece.shape[2]).T
        high = piece.astype(BF)
        f_ref[0] = high
        f_ref[1] = (piece - high.astype(jnp.float32)).astype(BF)
    width = o_ref.shape[2]
    step = 512
    for n in range(0, width, step):
        at = slice(n, n + step)
        rows = []
        for b, ref in enumerate(refs[:2]):
            rows.append(ref[0:half, at])
            if far and b == 1:
                rows.append(refs[2][:, at])
            else:
                rows.append(ref[half + TOP :, at])
        got = jnp.dot(chosen, jnp.concatenate(rows, axis=0), preferred_element_type=jnp.float32)
        o_ref[:, :, at] = got.astype(BF).reshape(DESTS, per, step)


def weighted(f_ref, rows):
    part = jnp.dot(f_ref[0], rows, preferred_element_type=jnp.float32)
    return part + jnp.dot(f_ref[1], rows, preferred_element_type=jnp.float32)


def combine_a_kernel(fb_ref, fa_ref, r_ref, own, c_top, c_low, a_top, a_low, b_top, b_low):
    half = 32
    width = r_ref.shape[2]
    near = 2 * SLOTS - LATE
    step = 512
    for n in range(0, width, step):
        at = slice(n, n + step)
        part = weighted(fb_ref, r_ref[:, 0:near, at].reshape(DESTS * near, step))
        own[:, at] = part[0 : 2 * half]
        c_top[:, at] = part[2 * half : 3 * half].astype(c_top.dtype)
        c_low[:, at] = part[3 * half :].astype(c_low.dtype)
        part = weighted(fa_ref, r_ref[:, near:, at].reshape(DESTS * 2 * SLOTS, step))
        for i, o in enumerate((a_top, a_low, b_top, b_low)):
            o[:, at] = part[i * half : (i + 1) * half].astype(o.dtype)


def combine_b_kernel(f_ref, r_ref, own_ref, out_ref):
    width = r_ref.shape[2]
    step = 512
    for n in range(0, width, step):
        at = slice(n, n + step)
        out_ref[:, at] = own_ref[:, at] + weighted(f_ref, r_ref[:, :, at].reshape(DESTS * LATE, step))


def join_kernel(at_top, one_ref, two_ref, over_ref, out_ref):
    half = over_ref.shape[0]
    total = (one_ref[...] + over_ref[...].astype(jnp.float32)).astype(BF)
    out_ref[0:half, :] = total if at_top else two_ref[...]
    out_ref[half:, :] = two_ref[...] if at_top else total


def up_kernel(off_ref, xa_ref, xb_ref, *refs):
    groups = refs[0:8]
    ha_ref, hn_ref, hl_ref, wg, wu, gate_s, sems = refs[8:]
    size = groups[0].shape[1]
    copies = [[], []]
    for which, dst in enumerate((wg, wu)):
        for i in range(8):
            at = pl.multiple_of(off_ref[i] * size, size)
            copies[which].append(
                pltpu.make_async_copy(
                    groups[i].at[which], dst.at[pl.ds(at, size), :], sems.at[which * 8 + i]
                )
            )
    for group in copies:
        for c in group:
            c.start()
    rows = xa_ref.shape[0]
    part = 8
    per = 2 * SLOTS
    step = part * per
    for c in copies[0]:
        c.wait()
    for j, x_ref in enumerate((xa_ref, xb_ref)):
        for r in range(0, rows, step):
            gate_s[j * rows + r : j * rows + r + step, :] = jnp.dot(
                x_ref[r : r + step, :], wg[...], preferred_element_type=jnp.float32
            )
    for c in copies[1]:
        c.wait()
    for j, x_ref in enumerate((xa_ref, xb_ref)):
        for k, r in enumerate(range(0, rows, step)):
            gate = gate_s[j * rows + r : j * rows + r + step, :]
            up = jnp.dot(x_ref[r : r + step, :], wu[...], preferred_element_type=jnp.float32)
            hidden = gate / (1.0 + jnp.exp(-gate)) * up
            if j == 0:
                ha_ref[r : r + step, :] = hidden.astype(BF)
            else:
                hidden = hidden.reshape(part, per, hidden.shape[1])
                near = part * (per - LATE)
                hn_ref[k * near : (k + 1) * near, :] = (
                    hidden[:, LATE:, :].reshape(near, hidden.shape[2]).astype(BF)
                )
                late = part * LATE
                hl_ref[k * late : (k + 1) * late, :] = (
                    hidden[:, 0:LATE, :].reshape(late, hidden.shape[2]).astype(BF)
                )


def down_kernel(count, off_ref, *refs):
    h_refs = refs[0:count]
    downs = refs[count : count + 8]
    o_ref, wd, done, sems, out_sems = refs[count + 8 :]
    size = downs[0].shape[1]
    outs = []
    copies = [pltpu.make_async_copy(downs[i], wd.at[i], sems.at[i]) for i in range(8)]
    for c in copies:
        c.start()
    part = 8
    for i in range(8):
        copies[i].wait()
        at = pl.ds(pl.multiple_of(off_ref[i] * size, size), size)
        first = 0
        for h_ref in h_refs:
            per = h_ref.shape[0] // DESTS
            for d in range(0, DESTS, part):
                got = jnp.dot(
                    h_ref[d * per : (d + part) * per, :], wd[i], preferred_element_type=jnp.float32
                )
                done[i, d : d + part, first : first + per, :] = got.reshape(part, per, size).astype(BF)
            first += per
        outs.append(pltpu.make_async_copy(done.at[i], o_ref.at[:, :, at], out_sems.at[i]))
        outs[i].start()
    for c in outs:
        c.wait()


def cost(flops, moved, hard=0):
    return pl.CostEstimate(flops=flops, bytes_accessed=moved, transcendentals=hard)


def shape(dims, kind=BF):
    return jax.ShapeDtypeStruct(dims, kind)


def exchange(value):
    return lax.all_to_all(value, ("x", "y"), split_axis=0, concat_axis=0, tiled=True)


def per_device(tokens, routes, route_weight, capacity, hot_expert, w_gate, w_up, w_down):
    zp, zq, core, zh = (lax.axis_index(n) for n in ("zp", "zq", "core", "zh"))
    ring = ("zp", "zh")
    order = [0, 2, 1, 3]
    fwd = [(order[i], order[(i + 1) % 4]) for i in range(4)]
    back = [(order[(i + 1) % 4], order[i]) for i in range(4)]
    swap = [(0, 1), (1, 0)]
    tok, width = tokens.shape
    half = tok // 2
    ff = w_gate.shape[2]
    piece = w_gate.shape[1]
    per = 2 * SLOTS
    rows = DESTS * per
    split = half + TOP

    scal = jnp.stack([zp, zh * 8 + zp]).astype(jnp.int32)
    own = pl.pallas_call(
        pack_kernel,
        out_shape=shape((tok + TOP, width)),
        in_specs=[VMEM] * 3,
        out_specs=VMEM,
        compiler_params=grant(8),
        cost_estimate=cost(0, 600 << 10),
        name="pack",
    )(tokens, routes.T, route_weight.T)
    tok3 = lax.ppermute(own, ring, back)
    tok1 = lax.ppermute(own, ring, fwd)
    mine_gu, other_gu, mine_d, other_d = pl.pallas_call(
        weights_kernel,
        out_shape=[shape((2, piece, ff)), shape((2, piece, ff)), shape((ff, piece)), shape((ff, piece))],
        in_specs=[SMEM, ANY, ANY, ANY],
        out_specs=[ANY] * 4,
        scratch_shapes=[
            pltpu.VMEM((2, 2, piece, ff), BF),
            pltpu.VMEM((2, ff, piece), BF),
            pltpu.SemaphoreType.DMA((6,)),
            pltpu.SemaphoreType.DMA((6,)),
        ],
        compiler_params=grant(56),
        cost_estimate=cost(0, 5 << 20),
        name="pack_weights",
    )(scal, w_gate, w_up, w_down)

    def shards(mine, other):
        a = lax.ppermute(other, "zp", swap)
        b = lax.ppermute(mine, "zq", swap)
        c = lax.ppermute(a, "zq", swap)
        near = [lax.ppermute(v, "core", swap) for v in (mine, a, b, c)]
        return [mine, a, b, c] + near

    gates_ups = shards(mine_gu, other_gu)
    downs = shards(mine_d, other_d)

    far_top = lax.ppermute(tok1[:split], ring, fwd)
    far_low = lax.ppermute(tok3[split:], ring, back)

    near = per - LATE

    def dispatch(factor_shapes, *blocks):
        return pl.pallas_call(
            functools.partial(dispatch_kernel, len(blocks) == 3),
            out_shape=[shape((DESTS, per, width))] + [shape((2,) + f) for f in factor_shapes],
            in_specs=[SMEM] * 3 + [VMEM] * len(blocks),
            out_specs=[VMEM] * (1 + len(factor_shapes)),
            compiler_params=grant(12),
            cost_estimate=cost(2 * rows * 2 * tok * width, 2 << 20),
        )(scal, capacity, hot_expert, *blocks)

    sent_b, fac_near, fac_late = dispatch([(2 * tok, DESTS * near), (tok, DESTS * LATE)], own, tok3)
    x_b = exchange(sent_b).reshape(rows, width)
    sent_a, fac_a = dispatch([(2 * tok, rows)], tok1, far_top, far_low)
    x_a = exchange(sent_a).reshape(rows, width)

    place = []
    for g in (0, 1):
        for b in (0, 1):
            for a in (0, 1):
                place.append((zp ^ a) * 4 + (zq ^ b) * 2 + (core ^ g))
    off = jnp.stack(place).astype(jnp.int32)
    h_a, h_near, h_late = pl.pallas_call(
        up_kernel,
        out_shape=[shape((n, ff)) for n in (rows, DESTS * near, DESTS * LATE)],
        in_specs=[SMEM, VMEM, VMEM] + [ANY] * 8,
        out_specs=[VMEM] * 3,
        scratch_shapes=[pltpu.VMEM((width, ff), BF)] * 2
        + [pltpu.VMEM((2 * rows, ff), jnp.float32), pltpu.SemaphoreType.DMA((16,))],
        compiler_params=grant(24),
        cost_estimate=cost(8 * rows * width * ff, 11 << 20, 2 * rows * ff),
        name="gate_up",
    )(off, x_a, x_b, *gates_ups)

    def down(*hs):
        count = sum(h.shape[0] for h in hs)
        return pl.pallas_call(
            functools.partial(down_kernel, len(hs)),
            out_shape=shape((DESTS, count // DESTS, width)),
            in_specs=[SMEM] + [VMEM] * len(hs) + [ANY] * 8,
            out_specs=ANY,
            scratch_shapes=[
                pltpu.VMEM((8, ff, piece), BF),
                pltpu.VMEM((8, DESTS, count // DESTS, piece), BF),
                pltpu.SemaphoreType.DMA((8,)),
                pltpu.SemaphoreType.DMA((8,)),
            ],
            compiler_params=grant(54),
            cost_estimate=cost(2 * count * width * ff, 6 << 20),
        )(off, *hs, *downs)

    def local(kernel, ins, outs, mib):
        return pl.pallas_call(
            kernel,
            out_shape=outs,
            in_specs=[VMEM] * len(ins),
            out_specs=[VMEM] * len(outs),
            compiler_params=grant(mib),
            cost_estimate=cost(1 << 20, 3 << 20),
        )(*ins)

    f32 = jnp.float32
    back_a = exchange(down(h_near, h_a))
    back_b = exchange(down(h_late))
    part0, p3_top, p3_low, p1_top, p1_low, p2_top, p2_low = local(
        combine_a_kernel,
        (fac_near, fac_a, back_a),
        [shape((tok, width), f32)] + [shape((half, width), k) for k in (BF, f32, f32, BF, BF, BF)],
        10,
    )
    over_back = lax.ppermute(p2_top, ring, back)
    over_fwd = lax.ppermute(p2_low, ring, fwd)
    block = [shape((tok, width))]
    (to_back,) = local(functools.partial(join_kernel, True), (p1_top, p1_low, over_back), block, 56)
    from_next = lax.ppermute(to_back, ring, back)
    (to_fwd,) = local(functools.partial(join_kernel, False), (p3_low, p3_top, over_fwd), block, 56)
    from_prev = lax.ppermute(to_fwd, ring, fwd)
    (part0,) = local(combine_b_kernel, (fac_late, back_b, part0), [shape((tok, width), f32)], 6)
    total = part0 + from_next.astype(f32) + from_prev.astype(f32)
    return total.astype(BF)


def solution(mesh):
    fine = Mesh(mesh.devices.reshape(2, 2, 2, 4, 2, 4), ("zp", "zq", "core", "x", "zh", "y"))
    dp, ex = ("zp", "zq", "core"), ("x", "zh", "y")
    in_specs = (
        P(dp + ex, None),
        P(dp + ex, None),
        P(dp + ex, None),
        P(),
        P(),
        P(ex, dp, None),
        P(ex, dp, None),
        P(ex, None, dp),
    )

    return jax.shard_map(
        per_device, mesh=fine, in_specs=in_specs, out_specs=P(dp + ex, None), check_vma=False
    )
```

```python
import functools
import jax
import jax.numpy as jnp
from jax import lax
from jax.sharding import Mesh, PartitionSpec as P
from jax.experimental import pallas as pl
from jax.experimental.pallas import tpu as pltpu

SLOTS = 12
EARLY = 4
LATE = SLOTS - EARLY
DESTS = 16
TOP = 8
GRANT_UP, GRANT_DOWN, GRANT_A, GRANT_B, GRANT_C = 54, 54, 10, 10, 6
BF = jnp.bfloat16
SMEM = pl.BlockSpec(memory_space=pltpu.SMEM)
VMEM = pl.BlockSpec(memory_space=pltpu.VMEM)
ANY = pl.BlockSpec(memory_space=pl.ANY)


def grant(mib):
    return pltpu.CompilerParams(vmem_limit_bytes=mib << 20)


def pack_kernel(t_ref, r_ref, w_ref, o_ref):
    half = t_ref.shape[0] // 2
    tok = t_ref.shape[0]
    o_ref[0:half, :] = t_ref[0:half, :]
    o_ref[half + TOP :, :] = t_ref[half:, :]
    weight = w_ref[...]
    high = weight // 256
    low = weight - high * 256
    gap = jnp.zeros((TOP, 128 - tok), jnp.float32)
    parts = []
    for v in (r_ref[...], high, low):
        parts += [v.astype(jnp.float32), gap]
    used = 128 * 3
    o_ref[half : half + TOP, 0:used] = jnp.concatenate(parts, axis=1).astype(BF)
    o_ref[half : half + TOP, used:] = jnp.zeros((TOP, t_ref.shape[1] - used), BF)


def weights_kernel(s_ref, g_ref, u_ref, d_ref, mgu, ogu, md, od, bgu, bd, sem_in, sem_out):
    zp = s_ref[0]
    loads, stores = [], []
    for which in (0, 1):
        e = zp if which == 0 else 1 - zp
        gu_out, d_out = ((mgu, md), (ogu, od))[which]
        for i, src in enumerate((g_ref, u_ref)):
            loads.append(pltpu.make_async_copy(src.at[e], bgu.at[which, i], sem_in.at[which * 3 + i]))
            stores.append(
                pltpu.make_async_copy(bgu.at[which, i], gu_out.at[i], sem_out.at[which * 3 + i])
            )
        loads.append(pltpu.make_async_copy(d_ref.at[e], bd.at[which], sem_in.at[which * 3 + 2]))
        stores.append(pltpu.make_async_copy(bd.at[which], d_out, sem_out.at[which * 3 + 2]))
    for c in loads:
        c.start()
    for a, b in zip(loads, stores):
        a.wait()
        b.start()
    for b in stores:
        b.wait()


def read_meta(ref, half, tok):
    rows = ref[half : half + TOP, 0:384].astype(jnp.float32)
    return rows[:, 0:tok], rows[:, 128 : 128 + tok] * 256.0 + rows[:, 256 : 256 + tok]


def plane_experts(s_ref, cap_ref, hot_ref, tok):
    base = s_ref[1]
    row = lax.broadcasted_iota(jnp.int32, (DESTS, tok), 0)
    expert = (row // 4) * 16 + (row % 4) * 2 + base
    limit = jnp.zeros((DESTS, tok), jnp.int32)
    for d in range(DESTS):
        e = (d // 4) * 16 + (d % 4) * 2 + base
        cap = jnp.where(e == hot_ref[0], SLOTS, cap_ref[e])
        limit = jnp.where(row == d, cap, limit)
    return expert.astype(jnp.float32), limit.astype(jnp.float32)


def slots_of(named_by, expert, limit, first, tok, turn=0):
    earlier = jnp.where(
        lax.broadcasted_iota(jnp.int32, (tok, tok), 0) < lax.broadcasted_iota(jnp.int32, (tok, tok), 1),
        1.0,
        0.0,
    ).astype(BF)
    named = named_by[0:1, :] == expert
    for k in range(1, TOP):
        named = jnp.logical_or(named, named_by[k : k + 1, :] == expert)
    rank = jnp.dot(jnp.where(named, 1.0, 0.0).astype(BF), earlier, preferred_element_type=jnp.float32)
    kept = jnp.logical_and(named, rank < limit)
    if turn:
        rank = jnp.where(rank < turn, rank + (SLOTS - turn), rank - turn)
    return jnp.where(kept, rank + first, -1.0).astype(jnp.int32)


def match_rows(slots, per, width):
    want = lax.broadcasted_iota(jnp.int32, (DESTS, per, width), 1)
    return want == slots[:, None, :]


def dispatch_kernel(far, s_ref, cap_ref, hot_ref, *refs):
    blocks = 3 if far else 2
    o_ref, factor_refs = refs[blocks], refs[blocks + 1 :]
    refs = refs[:blocks]
    half = 32
    tok = 2 * half
    per = o_ref.shape[1]
    expert, limit = plane_experts(s_ref, cap_ref, hot_ref, tok)
    slots, shares = [], []
    for b, ref in enumerate(refs[:2]):
        routes, weight = read_meta(ref, half, tok)
        turn = EARLY if b == 0 and not far else 0
        slots.append(slots_of(routes, expert, limit, b * SLOTS, tok, turn))
        share = weight / jnp.sum(weight, axis=0, keepdims=True)
        picked = jnp.zeros((DESTS, tok), jnp.float32)
        for k in range(TOP):
            picked = picked + jnp.where(routes[k : k + 1, :] == expert, share[k : k + 1, :], 0.0)
        shares.append(picked)
    slots = jnp.concatenate(slots, axis=1)
    shares = jnp.concatenate(shares, axis=1)
    match = match_rows(slots, per, 2 * tok)
    chosen = jnp.where(match, 1.0, 0.0).reshape(DESTS * per, 2 * tok).astype(BF)
    factor = jnp.where(match, shares[:, None, :], 0.0)
    pieces = [factor[:, LATE:, :], factor[:, 0:LATE, 0:tok]]
    for piece, f_ref in zip(pieces, factor_refs):
        piece = piece.reshape(-1, piece.shape[2]).T
        high = piece.astype(BF)
        f_ref[0] = high
        f_ref[1] = (piece - high.astype(jnp.float32)).astype(BF)
    width = o_ref.shape[2]
    step = 512
    for n in range(0, width, step):
        at = slice(n, n + step)
        rows = []
        for b, ref in enumerate(refs[:2]):
            rows.append(ref[0:half, at])
            if far and b == 1:
                rows.append(refs[2][:, at])
            else:
                rows.append(ref[half + TOP :, at])
        got = jnp.dot(chosen, jnp.concatenate(rows, axis=0), preferred_element_type=jnp.float32)
        o_ref[:, :, at] = got.astype(BF).reshape(DESTS, per, step)


def weighted(f_ref, rows):
    part = jnp.dot(f_ref[0], rows, preferred_element_type=jnp.float32)
    return part + jnp.dot(f_ref[1], rows, preferred_element_type=jnp.float32)


def combine_a_kernel(f_ref, r_ref, one, two_top, two_low):
    half = two_top.shape[0]
    width = r_ref.shape[2]
    step = 512
    for n in range(0, width, step):
        at = slice(n, n + step)
        part = weighted(f_ref, r_ref[:, :, at].reshape(-1, step))
        one[:, at] = part[0 : 2 * half]
        two_top[:, at] = part[2 * half : 3 * half].astype(BF)
        two_low[:, at] = part[3 * half :].astype(BF)


def combine_b_kernel(f_one, f_near, r_ref, one, over_back, over_fwd, own, to_back, to_fwd):
    half = over_back.shape[0]
    width = r_ref.shape[2]
    step = 512
    for n in range(0, width, step):
        at = slice(n, n + step)
        part = one[:, at] + weighted(f_one, r_ref[:, 0:LATE, at].reshape(-1, step))
        to_back[0:half, at] = (part[0:half] + over_back[:, at].astype(jnp.float32)).astype(BF)
        to_back[half:, at] = part[half:].astype(BF)
        part = weighted(f_near, r_ref[:, LATE:, at].reshape(-1, step))
        own[:, at] = part[0 : 2 * half]
        to_fwd[0:half, at] = part[2 * half : 3 * half].astype(BF)
        to_fwd[half:, at] = (part[3 * half :] + over_fwd[:, at].astype(jnp.float32)).astype(BF)


def combine_c_kernel(f_ref, r_ref, own_ref, out_ref):
    width = r_ref.shape[2]
    step = 512
    for n in range(0, width, step):
        at = slice(n, n + step)
        out_ref[:, at] = own_ref[:, at] + weighted(f_ref, r_ref[:, :, at].reshape(-1, step))


def up_kernel(off_ref, xa_ref, xb_ref, *refs):
    groups = refs[0:8]
    tails, heads = (refs[8], refs[10]), (refs[9], refs[11])
    wg, wu, gate_s, sems = refs[12:]
    size = groups[0].shape[1]
    copies = [[], []]
    for which, dst in enumerate((wg, wu)):
        for i in range(8):
            at = pl.multiple_of(off_ref[i] * size, size)
            copies[which].append(
                pltpu.make_async_copy(
                    groups[i].at[which], dst.at[pl.ds(at, size), :], sems.at[which * 8 + i]
                )
            )
    for group in copies:
        for c in group:
            c.start()
    rows = xa_ref.shape[0]
    part = 8
    per = 2 * SLOTS
    step = part * per
    for c in copies[0]:
        c.wait()
    for j, x_ref in enumerate((xa_ref, xb_ref)):
        for r in range(0, rows, step):
            gate_s[j * rows + r : j * rows + r + step, :] = jnp.dot(
                x_ref[r : r + step, :], wg[...], preferred_element_type=jnp.float32
            )
    for c in copies[1]:
        c.wait()
    for j, x_ref in enumerate((xa_ref, xb_ref)):
        for k, r in enumerate(range(0, rows, step)):
            gate = gate_s[j * rows + r : j * rows + r + step, :]
            up = jnp.dot(x_ref[r : r + step, :], wu[...], preferred_element_type=jnp.float32)
            hidden = gate / (1.0 + jnp.exp(-gate)) * up
            hidden = hidden.reshape(part, per, hidden.shape[1])
            tail = part * (per - LATE)
            tails[j][k * tail : (k + 1) * tail, :] = (
                hidden[:, LATE:, :].reshape(tail, hidden.shape[2]).astype(BF)
            )
            head = part * LATE
            heads[j][k * head : (k + 1) * head, :] = (
                hidden[:, 0:LATE, :].reshape(head, hidden.shape[2]).astype(BF)
            )


def down_kernel(count, off_ref, *refs):
    h_refs = refs[0:count]
    downs = refs[count : count + 8]
    o_ref, wd, done, sems, out_sems = refs[count + 8 :]
    size = downs[0].shape[1]
    outs = []
    copies = [pltpu.make_async_copy(downs[i], wd.at[i], sems.at[i]) for i in range(8)]
    for c in copies:
        c.start()
    part = 8
    for i in range(8):
        copies[i].wait()
        at = pl.ds(pl.multiple_of(off_ref[i] * size, size), size)
        first = 0
        for h_ref in h_refs:
            per = h_ref.shape[0] // DESTS
            for d in range(0, DESTS, part):
                got = jnp.dot(
                    h_ref[d * per : (d + part) * per, :], wd[i], preferred_element_type=jnp.float32
                )
                done[i, d : d + part, first : first + per, :] = got.reshape(part, per, size).astype(BF)
            first += per
        outs.append(pltpu.make_async_copy(done.at[i], o_ref.at[:, :, at], out_sems.at[i]))
        outs[i].start()
    for c in outs:
        c.wait()


def cost(flops, moved, hard=0):
    return pl.CostEstimate(flops=flops, bytes_accessed=moved, transcendentals=hard)


def shape(dims, kind=BF):
    return jax.ShapeDtypeStruct(dims, kind)


def exchange(value):
    return lax.all_to_all(value, ("x", "y"), split_axis=0, concat_axis=0, tiled=True)


def per_device(tokens, routes, route_weight, capacity, hot_expert, w_gate, w_up, w_down):
    zp, zq, core, zh = (lax.axis_index(n) for n in ("zp", "zq", "core", "zh"))
    ring = ("zp", "zh")
    order = [0, 2, 1, 3]
    fwd = [(order[i], order[(i + 1) % 4]) for i in range(4)]
    back = [(order[(i + 1) % 4], order[i]) for i in range(4)]
    swap = [(0, 1), (1, 0)]
    tok, width = tokens.shape
    half = tok // 2
    ff = w_gate.shape[2]
    piece = w_gate.shape[1]
    per = 2 * SLOTS
    rows = DESTS * per
    split = half + TOP

    scal = jnp.stack([zp, zh * 8 + zp]).astype(jnp.int32)
    own = pl.pallas_call(
        pack_kernel,
        out_shape=shape((tok + TOP, width)),
        in_specs=[VMEM] * 3,
        out_specs=VMEM,
        compiler_params=grant(56),
        cost_estimate=cost(0, 600 << 10),
        name="pack",
    )(tokens, routes.T, route_weight.T)
    tok3 = lax.ppermute(own, ring, back)
    tok1 = lax.ppermute(own, ring, fwd)
    mine_gu, other_gu, mine_d, other_d = pl.pallas_call(
        weights_kernel,
        out_shape=[shape((2, piece, ff)), shape((2, piece, ff)), shape((ff, piece)), shape((ff, piece))],
        in_specs=[SMEM, ANY, ANY, ANY],
        out_specs=[ANY] * 4,
        scratch_shapes=[
            pltpu.VMEM((2, 2, piece, ff), BF),
            pltpu.VMEM((2, ff, piece), BF),
            pltpu.SemaphoreType.DMA((6,)),
            pltpu.SemaphoreType.DMA((6,)),
        ],
        compiler_params=grant(56),
        cost_estimate=cost(0, 5 << 20),
        name="pack_weights",
    )(scal, w_gate, w_up, w_down)

    def shards(mine, other):
        a = lax.ppermute(other, "zp", swap)
        b = lax.ppermute(mine, "zq", swap)
        c = lax.ppermute(a, "zq", swap)
        near = [lax.ppermute(v, "core", swap) for v in (mine, a, b, c)]
        return [mine, a, b, c] + near

    gates_ups = shards(mine_gu, other_gu)
    downs = shards(mine_d, other_d)

    far_top = lax.ppermute(tok1[:split], ring, fwd)
    far_low = lax.ppermute(tok3[split:], ring, back)

    near = per - LATE

    def dispatch(factor_shapes, *blocks):
        return pl.pallas_call(
            functools.partial(dispatch_kernel, len(blocks) == 3),
            out_shape=[shape((DESTS, per, width))] + [shape((2,) + f) for f in factor_shapes],
            in_specs=[SMEM] * 3 + [VMEM] * len(blocks),
            out_specs=[VMEM] * (1 + len(factor_shapes)),
            compiler_params=grant(12),
            cost_estimate=cost(2 * rows * 2 * tok * width, 2 << 20),
        )(scal, capacity, hot_expert, *blocks)

    split_factors = [(2 * tok, DESTS * near), (tok, DESTS * LATE)]
    sent_b, fac_near, fac_late = dispatch(split_factors, own, tok3)
    x_b = exchange(sent_b).reshape(rows, width)
    sent_a, fac_two, fac_one = dispatch(split_factors, tok1, far_top, far_low)
    x_a = exchange(sent_a).reshape(rows, width)

    place = []
    for g in (0, 1):
        for b in (0, 1):
            for a in (0, 1):
                place.append((zp ^ a) * 4 + (zq ^ b) * 2 + (core ^ g))
    off = jnp.stack(place).astype(jnp.int32)
    h_two, h_one, h_near, h_late = pl.pallas_call(
        up_kernel,
        out_shape=[shape((n, ff)) for n in (DESTS * near, DESTS * LATE) * 2],
        in_specs=[SMEM, VMEM, VMEM] + [ANY] * 8,
        out_specs=[VMEM] * 4,
        scratch_shapes=[pltpu.VMEM((width, ff), BF)] * 2
        + [pltpu.VMEM((2 * rows, ff), jnp.float32), pltpu.SemaphoreType.DMA((16,))],
        compiler_params=grant(GRANT_UP),
        cost_estimate=cost(8 * rows * width * ff, 11 << 20, 2 * rows * ff),
        name="gate_up",
    )(off, x_a, x_b, *gates_ups)

    def down(*hs):
        count = sum(h.shape[0] for h in hs)
        return pl.pallas_call(
            functools.partial(down_kernel, len(hs)),
            out_shape=shape((DESTS, count // DESTS, width)),
            in_specs=[SMEM] + [VMEM] * len(hs) + [ANY] * 8,
            out_specs=ANY,
            scratch_shapes=[
                pltpu.VMEM((8, ff, piece), BF),
                pltpu.VMEM((8, DESTS, count // DESTS, piece), BF),
                pltpu.SemaphoreType.DMA((8,)),
                pltpu.SemaphoreType.DMA((8,)),
            ],
            compiler_params=grant(GRANT_DOWN),
            cost_estimate=cost(2 * count * width * ff, 6 << 20),
        )(off, *hs, *downs)

    def local(kernel, ins, outs, mib):
        return pl.pallas_call(
            kernel,
            out_shape=outs,
            in_specs=[VMEM] * len(ins),
            out_specs=[VMEM] * len(outs),
            compiler_params=grant(mib),
            cost_estimate=cost(1 << 20, 3 << 20),
        )(*ins)

    f32 = jnp.float32
    back_a = exchange(down(h_two))
    back_b = exchange(down(h_one, h_near))
    back_c = exchange(down(h_late))
    block, some, whole = shape((tok, width)), shape((half, width)), shape((tok, width), f32)
    one, two_top, two_low = local(combine_a_kernel, (fac_two, back_a), [whole, some, some], GRANT_A)
    over_back = lax.ppermute(two_top, ring, back)
    over_fwd = lax.ppermute(two_low, ring, fwd)
    part0, to_back, to_fwd = local(
        combine_b_kernel,
        (fac_one, fac_near, back_b, one, over_back, over_fwd),
        [whole, block, block],
        GRANT_B,
    )
    from_next = lax.ppermute(to_back, ring, back)
    from_prev = lax.ppermute(to_fwd, ring, fwd)
    (part0,) = local(combine_c_kernel, (fac_late, back_c, part0), [whole], GRANT_C)
    total = part0 + from_next.astype(f32) + from_prev.astype(f32)
    return total.astype(BF)


def solution(mesh):
    fine = Mesh(mesh.devices.reshape(2, 2, 2, 4, 2, 4), ("zp", "zq", "core", "x", "zh", "y"))
    dp, ex = ("zp", "zq", "core"), ("x", "zh", "y")
    in_specs = (
        P(dp + ex, None),
        P(dp + ex, None),
        P(dp + ex, None),
        P(),
        P(),
        P(ex, dp, None),
        P(ex, dp, None),
        P(ex, None, dp),
    )

    return jax.shard_map(
        per_device, mesh=fine, in_specs=in_specs, out_specs=P(dp + ex, None), check_vma=False
    )
```

```python
import functools
import jax
import jax.numpy as jnp
from jax import lax
from jax.sharding import Mesh, PartitionSpec as P
from jax.experimental import pallas as pl
from jax.experimental.pallas import tpu as pltpu

SLOTS = 12
EARLY = 4
LATE = SLOTS - EARLY
DESTS = 16
TOP = 8
GRANT_UP, GRANT_DOWN, GRANT_A, GRANT_B, GRANT_C = 54, 54, 10, 10, 6
BF = jnp.bfloat16
SMEM = pl.BlockSpec(memory_space=pltpu.SMEM)
VMEM = pl.BlockSpec(memory_space=pltpu.VMEM)
ANY = pl.BlockSpec(memory_space=pl.ANY)


def grant(mib):
    return pltpu.CompilerParams(vmem_limit_bytes=mib << 20)


def pack_kernel(t_ref, r_ref, w_ref, o_ref):
    half = t_ref.shape[0] // 2
    tok = t_ref.shape[0]
    o_ref[0:half, :] = t_ref[0:half, :]
    o_ref[half + TOP :, :] = t_ref[half:, :]
    weight = w_ref[...]
    high = weight // 256
    low = weight - high * 256
    gap = jnp.zeros((TOP, 128 - tok), jnp.float32)
    parts = []
    for v in (r_ref[...], high, low):
        parts += [v.astype(jnp.float32), gap]
    used = 128 * 3
    o_ref[half : half + TOP, 0:used] = jnp.concatenate(parts, axis=1).astype(BF)
    o_ref[half : half + TOP, used:] = jnp.zeros((TOP, t_ref.shape[1] - used), BF)


def weights_kernel(s_ref, g_ref, u_ref, d_ref, mgu, ogu, md, od, bgu, bd, sem_in, sem_out):
    zp = s_ref[0]
    loads, stores = [], []
    for which in (0, 1):
        e = zp if which == 0 else 1 - zp
        gu_out, d_out = ((mgu, md), (ogu, od))[which]
        for i, src in enumerate((g_ref, u_ref)):
            loads.append(pltpu.make_async_copy(src.at[e], bgu.at[which, i], sem_in.at[which * 3 + i]))
            stores.append(
                pltpu.make_async_copy(bgu.at[which, i], gu_out.at[i], sem_out.at[which * 3 + i])
            )
        loads.append(pltpu.make_async_copy(d_ref.at[e], bd.at[which], sem_in.at[which * 3 + 2]))
        stores.append(pltpu.make_async_copy(bd.at[which], d_out, sem_out.at[which * 3 + 2]))
    for c in loads:
        c.start()
    for a, b in zip(loads, stores):
        a.wait()
        b.start()
    for b in stores:
        b.wait()


def read_meta(ref, half, tok):
    rows = ref[half : half + TOP, 0:384].astype(jnp.float32)
    return rows[:, 0:tok], rows[:, 128 : 128 + tok] * 256.0 + rows[:, 256 : 256 + tok]


def plane_experts(s_ref, cap_ref, hot_ref, tok):
    base = s_ref[1]
    row = lax.broadcasted_iota(jnp.int32, (DESTS, tok), 0)
    expert = (row // 4) * 16 + (row % 4) * 2 + base
    limit = jnp.zeros((DESTS, tok), jnp.int32)
    for d in range(DESTS):
        e = (d // 4) * 16 + (d % 4) * 2 + base
        cap = jnp.where(e == hot_ref[0], SLOTS, cap_ref[e])
        limit = jnp.where(row == d, cap, limit)
    return expert.astype(jnp.float32), limit.astype(jnp.float32)


def slots_of(named_by, expert, limit, first, tok, turn=0):
    earlier = jnp.where(
        lax.broadcasted_iota(jnp.int32, (tok, tok), 0) < lax.broadcasted_iota(jnp.int32, (tok, tok), 1),
        1.0,
        0.0,
    ).astype(BF)
    named = named_by[0:1, :] == expert
    for k in range(1, TOP):
        named = jnp.logical_or(named, named_by[k : k + 1, :] == expert)
    rank = jnp.dot(jnp.where(named, 1.0, 0.0).astype(BF), earlier, preferred_element_type=jnp.float32)
    kept = jnp.logical_and(named, rank < limit)
    if turn:
        rank = jnp.where(rank < turn, rank + (SLOTS - turn), rank - turn)
    return jnp.where(kept, rank + first, -1.0).astype(jnp.int32)


def match_rows(slots, per, width):
    want = lax.broadcasted_iota(jnp.int32, (DESTS, per, width), 1)
    return want == slots[:, None, :]


def dispatch_kernel(far, s_ref, cap_ref, hot_ref, *refs):
    blocks = 3 if far else 2
    o_ref, factor_refs = refs[blocks], refs[blocks + 1 :]
    refs = refs[:blocks]
    half = 32
    tok = 2 * half
    per = o_ref.shape[1]
    expert, limit = plane_experts(s_ref, cap_ref, hot_ref, tok)
    slots, shares = [], []
    for b, ref in enumerate(refs[:2]):
        routes, weight = read_meta(ref, half, tok)
        turn = EARLY if b == 0 and not far else 0
        slots.append(slots_of(routes, expert, limit, b * SLOTS, tok, turn))
        share = weight / jnp.sum(weight, axis=0, keepdims=True)
        picked = jnp.zeros((DESTS, tok), jnp.float32)
        for k in range(TOP):
            picked = picked + jnp.where(routes[k : k + 1, :] == expert, share[k : k + 1, :], 0.0)
        shares.append(picked)
    slots = jnp.concatenate(slots, axis=1)
    shares = jnp.concatenate(shares, axis=1)
    match = match_rows(slots, per, 2 * tok)
    chosen = jnp.where(match, 1.0, 0.0).reshape(DESTS * per, 2 * tok).astype(BF)
    factor = jnp.where(match, shares[:, None, :], 0.0)
    pieces = [factor[:, LATE:, :], factor[:, 0:LATE, 0:tok]]
    for piece, f_ref in zip(pieces, factor_refs):
        piece = piece.reshape(-1, piece.shape[2]).T
        high = piece.astype(BF)
        f_ref[0] = high
        f_ref[1] = (piece - high.astype(jnp.float32)).astype(BF)
    width = o_ref.shape[2]
    step = 512
    for n in range(0, width, step):
        at = slice(n, n + step)
        rows = []
        for b, ref in enumerate(refs[:2]):
            rows.append(ref[0:half, at])
            if far and b == 1:
                rows.append(refs[2][:, at])
            else:
                rows.append(ref[half + TOP :, at])
        got = jnp.dot(chosen, jnp.concatenate(rows, axis=0), preferred_element_type=jnp.float32)
        o_ref[:, :, at] = got.astype(BF).reshape(DESTS, per, step)


def weighted(f_ref, rows):
    part = jnp.dot(f_ref[0], rows, preferred_element_type=jnp.float32)
    return part + jnp.dot(f_ref[1], rows, preferred_element_type=jnp.float32)


def combine_a_kernel(f_ref, r_ref, one, two_top, two_low):
    half = two_top.shape[0]
    width = r_ref.shape[2]
    step = 512
    for n in range(0, width, step):
        at = slice(n, n + step)
        part = weighted(f_ref, r_ref[:, :, at].reshape(-1, step))
        one[:, at] = part[0 : 2 * half]
        two_top[:, at] = part[2 * half : 3 * half].astype(BF)
        two_low[:, at] = part[3 * half :].astype(BF)


def combine_b_kernel(f_one, f_near, r_ref, one, over_back, over_fwd, own, to_back, to_fwd):
    half = over_back.shape[0]
    width = r_ref.shape[2]
    step = 512
    for n in range(0, width, step):
        at = slice(n, n + step)
        part = one[:, at] + weighted(f_one, r_ref[:, 0:LATE, at].reshape(-1, step))
        to_back[0:half, at] = (part[0:half] + over_back[:, at].astype(jnp.float32)).astype(BF)
        to_back[half:, at] = part[half:].astype(BF)
        part = weighted(f_near, r_ref[:, LATE:, at].reshape(-1, step))
        own[:, at] = part[0 : 2 * half]
        to_fwd[0:half, at] = part[2 * half : 3 * half].astype(BF)
        to_fwd[half:, at] = (part[3 * half :] + over_fwd[:, at].astype(jnp.float32)).astype(BF)


def combine_c_kernel(f_ref, r_ref, own_ref, out_ref):
    width = r_ref.shape[2]
    step = 512
    for n in range(0, width, step):
        at = slice(n, n + step)
        out_ref[:, at] = own_ref[:, at] + weighted(f_ref, r_ref[:, :, at].reshape(-1, step))


def up_kernel(off_ref, xa_ref, xb_ref, *refs):
    groups = refs[0:8]
    tails, heads = (refs[8], refs[10]), (refs[9], refs[11])
    wg, wu, gate_s, sems = refs[12:]
    size = groups[0].shape[1]
    copies = [[], []]
    for which, dst in enumerate((wg, wu)):
        for i in range(8):
            at = pl.multiple_of(off_ref[i] * size, size)
            copies[which].append(
                pltpu.make_async_copy(
                    groups[i].at[which], dst.at[pl.ds(at, size), :], sems.at[which * 8 + i]
                )
            )
    for group in copies:
        for c in group:
            c.start()
    rows = xa_ref.shape[0]
    part = 8
    per = 2 * SLOTS
    step = part * per
    for c in copies[0]:
        c.wait()
    for j, x_ref in enumerate((xa_ref, xb_ref)):
        for r in range(0, rows, step):
            gate_s[j * rows + r : j * rows + r + step, :] = jnp.dot(
                x_ref[r : r + step, :], wg[...], preferred_element_type=jnp.float32
            )
    for c in copies[1]:
        c.wait()
    for j, x_ref in enumerate((xa_ref, xb_ref)):
        for k, r in enumerate(range(0, rows, step)):
            gate = gate_s[j * rows + r : j * rows + r + step, :]
            up = jnp.dot(x_ref[r : r + step, :], wu[...], preferred_element_type=jnp.float32)
            hidden = gate / (1.0 + jnp.exp(-gate)) * up
            hidden = hidden.reshape(part, per, hidden.shape[1])
            tail = part * (per - LATE)
            tails[j][k * tail : (k + 1) * tail, :] = (
                hidden[:, LATE:, :].reshape(tail, hidden.shape[2]).astype(BF)
            )
            head = part * LATE
            heads[j][k * head : (k + 1) * head, :] = (
                hidden[:, 0:LATE, :].reshape(head, hidden.shape[2]).astype(BF)
            )


def down_kernel(count, off_ref, *refs):
    h_refs = refs[0:count]
    downs = refs[count : count + 8]
    o_ref, wd, done, sems, out_sems = refs[count + 8 : count + 13]
    kept = refs[count + 13 : 2 * count + 13]
    row_sems = refs[2 * count + 13]
    size = downs[0].shape[1]
    outs = []
    rows = [pltpu.make_async_copy(h_refs[j], kept[j], row_sems.at[j]) for j in range(count)]
    for c in rows:
        c.start()
    copies = [pltpu.make_async_copy(downs[i], wd.at[i], sems.at[i]) for i in range(8)]
    for c in copies:
        c.start()
    for c in rows:
        c.wait()
    part = 8
    for i in range(8):
        copies[i].wait()
        at = pl.ds(pl.multiple_of(off_ref[i] * size, size), size)
        first = 0
        for h_ref in kept:
            per = h_ref.shape[0] // DESTS
            for d in range(0, DESTS, part):
                got = jnp.dot(
                    h_ref[d * per : (d + part) * per, :], wd[i], preferred_element_type=jnp.float32
                )
                done[i, d : d + part, first : first + per, :] = got.reshape(part, per, size).astype(BF)
            first += per
        outs.append(pltpu.make_async_copy(done.at[i], o_ref.at[:, :, at], out_sems.at[i]))
        outs[i].start()
    for c in outs:
        c.wait()


def cost(flops, moved, hard=0):
    return pl.CostEstimate(flops=flops, bytes_accessed=moved, transcendentals=hard)


def shape(dims, kind=BF):
    return jax.ShapeDtypeStruct(dims, kind)


def exchange(value):
    return lax.all_to_all(value, ("x", "y"), split_axis=0, concat_axis=0, tiled=True)


def per_device(tokens, routes, route_weight, capacity, hot_expert, w_gate, w_up, w_down):
    zp, zq, core, zh = (lax.axis_index(n) for n in ("zp", "zq", "core", "zh"))
    ring = ("zp", "zh")
    order = [0, 2, 1, 3]
    fwd = [(order[i], order[(i + 1) % 4]) for i in range(4)]
    back = [(order[(i + 1) % 4], order[i]) for i in range(4)]
    swap = [(0, 1), (1, 0)]
    tok, width = tokens.shape
    half = tok // 2
    ff = w_gate.shape[2]
    piece = w_gate.shape[1]
    per = 2 * SLOTS
    rows = DESTS * per
    split = half + TOP

    scal = jnp.stack([zp, zh * 8 + zp]).astype(jnp.int32)
    own = pl.pallas_call(
        pack_kernel,
        out_shape=shape((tok + TOP, width)),
        in_specs=[VMEM] * 3,
        out_specs=VMEM,
        compiler_params=grant(56),
        cost_estimate=cost(0, 600 << 10),
        name="pack",
    )(tokens, routes.T, route_weight.T)
    tok3 = lax.ppermute(own, ring, back)
    tok1 = lax.ppermute(own, ring, fwd)
    mine_gu, other_gu, mine_d, other_d = pl.pallas_call(
        weights_kernel,
        out_shape=[shape((2, piece, ff)), shape((2, piece, ff)), shape((ff, piece)), shape((ff, piece))],
        in_specs=[SMEM, ANY, ANY, ANY],
        out_specs=[ANY] * 4,
        scratch_shapes=[
            pltpu.VMEM((2, 2, piece, ff), BF),
            pltpu.VMEM((2, ff, piece), BF),
            pltpu.SemaphoreType.DMA((6,)),
            pltpu.SemaphoreType.DMA((6,)),
        ],
        compiler_params=grant(56),
        cost_estimate=cost(0, 5 << 20),
        name="pack_weights",
    )(scal, w_gate, w_up, w_down)

    def shards(mine, other):
        a = lax.ppermute(other, "zp", swap)
        b = lax.ppermute(mine, "zq", swap)
        c = lax.ppermute(a, "zq", swap)
        near = [lax.ppermute(v, "core", swap) for v in (mine, a, b, c)]
        return [mine, a, b, c] + near

    gates_ups = shards(mine_gu, other_gu)
    downs = shards(mine_d, other_d)

    far_top = lax.ppermute(tok1[:split], ring, fwd)
    far_low = lax.ppermute(tok3[split:], ring, back)

    near = per - LATE

    def dispatch(factor_shapes, *blocks):
        return pl.pallas_call(
            functools.partial(dispatch_kernel, len(blocks) == 3),
            out_shape=[shape((DESTS, per, width))] + [shape((2,) + f) for f in factor_shapes],
            in_specs=[SMEM] * 3 + [VMEM] * len(blocks),
            out_specs=[VMEM] * (1 + len(factor_shapes)),
            compiler_params=grant(54 if len(blocks) == 3 else 12),
            cost_estimate=cost(2 * rows * 2 * tok * width, 2 << 20),
        )(scal, capacity, hot_expert, *blocks)

    split_factors = [(2 * tok, DESTS * near), (tok, DESTS * LATE)]
    sent_b, fac_near, fac_late = dispatch(split_factors, own, tok3)
    x_b = exchange(sent_b).reshape(rows, width)
    sent_a, fac_two, fac_one = dispatch(split_factors, tok1, far_top, far_low)
    x_a = exchange(sent_a).reshape(rows, width)

    place = []
    for g in (0, 1):
        for b in (0, 1):
            for a in (0, 1):
                place.append((zp ^ a) * 4 + (zq ^ b) * 2 + (core ^ g))
    off = jnp.stack(place).astype(jnp.int32)
    h_two, h_one, h_near, h_late = pl.pallas_call(
        up_kernel,
        out_shape=[shape((n, ff)) for n in (DESTS * near, DESTS * LATE) * 2],
        in_specs=[SMEM, VMEM, VMEM] + [ANY] * 8,
        out_specs=[VMEM] * 4,
        scratch_shapes=[pltpu.VMEM((width, ff), BF)] * 2
        + [pltpu.VMEM((2 * rows, ff), jnp.float32), pltpu.SemaphoreType.DMA((16,))],
        compiler_params=grant(GRANT_UP),
        cost_estimate=cost(8 * rows * width * ff, 11 << 20, 2 * rows * ff),
        name="gate_up",
    )(off, x_a, x_b, *gates_ups)

    def down(*hs):
        count = sum(h.shape[0] for h in hs)
        return pl.pallas_call(
            functools.partial(down_kernel, len(hs)),
            out_shape=shape((DESTS, count // DESTS, width)),
            in_specs=[SMEM] + [ANY] * len(hs) + [ANY] * 8,
            out_specs=ANY,
            scratch_shapes=[
                pltpu.VMEM((8, ff, piece), BF),
                pltpu.VMEM((8, DESTS, count // DESTS, piece), BF),
                pltpu.SemaphoreType.DMA((8,)),
                pltpu.SemaphoreType.DMA((8,)),
            ]
            + [pltpu.VMEM(h.shape, BF) for h in hs]
            + [pltpu.SemaphoreType.DMA((len(hs),))],
            compiler_params=grant(GRANT_DOWN),
            cost_estimate=cost(2 * count * width * ff, 6 << 20),
        )(off, *hs, *downs)

    def local(kernel, ins, outs, mib):
        return pl.pallas_call(
            kernel,
            out_shape=outs,
            in_specs=[VMEM] * len(ins),
            out_specs=[VMEM] * len(outs),
            compiler_params=grant(mib),
            cost_estimate=cost(1 << 20, 3 << 20),
        )(*ins)

    f32 = jnp.float32
    back_a = exchange(down(h_two))
    back_b = exchange(down(h_one, h_near))
    back_c = exchange(down(h_late))
    block, some, whole = shape((tok, width)), shape((half, width)), shape((tok, width), f32)
    one, two_top, two_low = local(combine_a_kernel, (fac_two, back_a), [whole, some, some], GRANT_A)
    over_back = lax.ppermute(two_top, ring, back)
    over_fwd = lax.ppermute(two_low, ring, fwd)
    part0, to_back, to_fwd = local(
        combine_b_kernel,
        (fac_one, fac_near, back_b, one, over_back, over_fwd),
        [whole, block, block],
        GRANT_B,
    )
    from_next = lax.ppermute(to_back, ring, back)
    from_prev = lax.ppermute(to_fwd, ring, fwd)
    (part0,) = local(combine_c_kernel, (fac_late, back_c, part0), [whole], GRANT_C)
    total = part0 + from_next.astype(f32) + from_prev.astype(f32)
    return total.astype(BF)


def solution(mesh):
    fine = Mesh(mesh.devices.reshape(2, 2, 2, 4, 2, 4), ("zp", "zq", "core", "x", "zh", "y"))
    dp, ex = ("zp", "zq", "core"), ("x", "zh", "y")
    in_specs = (
        P(dp + ex, None),
        P(dp + ex, None),
        P(dp + ex, None),
        P(),
        P(),
        P(ex, dp, None),
        P(ex, dp, None),
        P(ex, None, dp),
    )

    return jax.shard_map(
        per_device, mesh=fine, in_specs=in_specs, out_specs=P(dp + ex, None), check_vma=False
    )
```
